512 devices in a mesh: dp: 4 (over x), expert: 128 (over y, z, core).
Axes of the slice: x: 4, y: 8, z: 8, core: 2. Of those that a mesh axis runs over, the one named last changes fastest.
Arguments:
- tokens: bfloat16 [65536, 512], P(('dp', 'expert')), may hold values from -6 to 6
- codes: int32 [65536, 2], P(('dp', 'expert')), may hold values from 0 to 127, as said below
- cotangent: bfloat16 [65536, 512], P(('dp', 'expert')), may hold values from -6 to 6
- w_gate: bfloat16 [128, 512, 1024], P('expert'), may hold values from -0.25 to 0.25
- w_up: bfloat16 [128, 512, 1024], P('expert'), may hold values from -0.25 to 0.25
- w_down: bfloat16 [128, 1024, 512], P('expert'), may hold values from -0.1875 to 0.1875
Outputs:
- head_output: bfloat16 [65536, 512], P(('dp', 'expert'))
- grad_tokens: bfloat16 [65536, 512], P(('dp', 'expert'))
- grad_gate: bfloat16 [128, 512, 1024], P('expert', None, 'dp')
- grad_up: bfloat16 [128, 512, 1024], P('expert', None, 'dp')
- grad_down: bfloat16 [128, 1024, 512], P('expert', 'dp')
The draws below stay inside these ranges and needn't reach their ends.
Inputs may be any that keep to these rules, and one draw needn't show every extreme that they name: A token's two codes differ. Within each device's 128 tokens (aligned blocks of 128 rows), each arm is named at most 4 times over both columns, and one arm, the same for every block, is named exactly 4 times in every block.
All inputs are finite; a program needn't handle non-finite values.
Results may differ from the reference program's by a relative error of at most 0.009.
Values may be sent and summed in bfloat16 or wider, within the bound.
A program may use at most 64 MiB of HBM per device.

```python
import jax
import jax.numpy as jnp
from jax import lax

DW = 512
HW = 1024
TOK_DEV = 128
E = 128
CAP = 4
TOKENS = 65536
N_DP = 4
N_EXPERT = 128


def draw_codes(key, part):
    block_count = TOKENS // TOK_DEV
    hot_arm = jax.random.randint(jax.random.fold_in(key, 7), (), 0, E).astype(jnp.int32)
    other_slots = (E - 1) * CAP
    picked_count = 2 * TOK_DEV - CAP

    def one_block(block_key):
        sub_keys = jax.random.split(block_key, 4)
        slot_order = jax.random.permutation(sub_keys[0], other_slots)
        chosen = slot_order < picked_count
        picked = jnp.nonzero(chosen, size=picked_count)[0]
        inner_ids = jnp.concatenate([jnp.zeros((CAP,), jnp.int32), (picked // CAP + 1).astype(jnp.int32)])
        others = (hot_arm + 1 + jax.random.permutation(sub_keys[1], E - 1).astype(jnp.int32)) % E
        labels = jnp.concatenate([hot_arm[None], others]).astype(jnp.int32)
        arm_list = labels[inner_ids]
        code_pairs = jnp.stack([arm_list[:TOK_DEV], arm_list[TOK_DEV:]], axis=1)
        swap_bits = jax.random.randint(sub_keys[2], (TOK_DEV, 1), 0, 2)
        code_pairs = jnp.where(swap_bits == 1, code_pairs[:, ::-1], code_pairs)
        shuffle = jax.random.permutation(sub_keys[3], TOK_DEV)
        return code_pairs[shuffle]
    block_keys = jax.vmap(lambda block_index: jax.random.fold_in(key, block_index))(jnp.arange(block_count))
    return jax.vmap(one_block)(block_keys).reshape(TOKENS, 2).astype(jnp.int32)


def block_scale(key, extent, pieces, smallest, high):
    def one(dim, shards_of):
        draws = jax.random.uniform(jax.random.fold_in(jax.random.fold_in(key, 6), dim), (shards_of,), jnp.float32, smallest / len(pieces), high / len(pieces))
        return jnp.repeat(jnp.exp(draws), extent[dim] // shards_of).reshape((-1,) + (1,) * (len(extent) - dim - 1))

    factor_of = one(*pieces[0])
    for cut in pieces[1:]:
        factor_of = factor_of * one(*cut)
    return factor_of


def scatter_about(key, shape, spread, bound, cuts=(), kind=jnp.bfloat16):
    values = spread * jax.random.normal(key, shape, jnp.float32)
    if cuts:
        values = values * block_scale(key, shape, cuts, -0.22, 0.18)
    return jnp.clip(values, -bound, bound).astype(kind)


def setup_inputs(seed: int = 0) -> dict:
    keys = jax.random.split(jax.random.key(seed), 7)
    return {
        "tokens": scatter_about(keys[0], (TOKENS, DW), 1.0, 6.0, ((0, 512),)),
        "codes": draw_codes(jax.random.fold_in(keys[6], 71), 0),
        "cotangent": scatter_about(keys[2], (TOKENS, DW), 1.0, 6.0, ((0, 512),)),
        "w_gate": scatter_about(keys[3], (E, DW, HW), DW ** -0.5, 0.25, ((0, 128),)),
        "w_up": scatter_about(keys[4], (E, DW, HW), DW ** -0.5, 0.25, ((0, 128),)),
        "w_down": scatter_about(keys[5], (E, HW, DW), HW ** -0.5, 0.1875, ((0, 128),)),
    }


fact_share = 0.7
counter_share = 0.3


def rounded(value):
    return lax.optimization_barrier(value.astype(jnp.bfloat16)).astype(jnp.float32)


def arm_pass(operands):
    arm_tokens, arm_cot, gate_w, up_w, down_w = operands
    tok_f = arm_tokens.astype(jnp.float32)
    cot_f = arm_cot.astype(jnp.float32)
    gate_f = gate_w.astype(jnp.float32)
    up_f = up_w.astype(jnp.float32)
    down_f = down_w.astype(jnp.float32)
    gate_pre = jnp.einsum("prc,ch->prh", tok_f, gate_f)
    up_pre = jnp.einsum("prc,ch->prh", tok_f, up_f)
    sigmoid_gate = jax.nn.sigmoid(gate_pre)
    activated = gate_pre * sigmoid_gate
    hidden = (activated * up_pre).astype(jnp.bfloat16)
    hidden_f = hidden.astype(jnp.float32)
    out_rows = jnp.einsum("prh,hc->prc", hidden_f, down_f).astype(jnp.bfloat16)
    d_hidden = jnp.einsum("prc,hc->prh", cot_f, down_f)
    d_up = (d_hidden * activated).astype(jnp.bfloat16).astype(jnp.float32)
    silu_slope = sigmoid_gate * (1.0 + gate_pre * (1.0 - sigmoid_gate))
    d_gate = (d_hidden * up_pre * silu_slope).astype(jnp.bfloat16).astype(jnp.float32)
    input_rows = (jnp.einsum("prh,ch->prc", d_gate, gate_f) + jnp.einsum("prh,ch->prc", d_up, up_f)).astype(jnp.bfloat16)
    grad_gate = jnp.sum(rounded(jnp.einsum("prc,prh->pch", tok_f, d_gate)), axis=0).astype(jnp.bfloat16)
    grad_up = jnp.sum(rounded(jnp.einsum("prc,prh->pch", tok_f, d_up)), axis=0).astype(jnp.bfloat16)
    grad_down = jnp.sum(rounded(jnp.einsum("prh,prc->phc", hidden_f, cot_f)), axis=0).astype(jnp.bfloat16)
    return out_rows, input_rows, grad_gate, grad_up, grad_down


def reference(tokens, codes, cotangent, w_gate, w_up, w_down):
    block_count = TOKENS // TOK_DEV
    flat_codes = codes.reshape(block_count, 2 * TOK_DEV).astype(jnp.int32)
    arm_ids = jnp.arange(E, dtype=jnp.int32)
    onehot = (flat_codes[:, :, None] == arm_ids[None, None, :]).astype(jnp.int32)
    earlier = jnp.cumsum(onehot, axis=1) - onehot
    destination = (flat_codes * CAP + jnp.sum(earlier * onehot, axis=2)).astype(jnp.int32)
    shares = jnp.tile(jnp.array([fact_share, counter_share], jnp.float32), TOK_DEV)
    token_rows = jnp.repeat(tokens.reshape(block_count, TOK_DEV, DW), 2, axis=1)
    cot_rows = (jnp.repeat(cotangent.reshape(block_count, TOK_DEV, DW).astype(jnp.float32), 2, axis=1) * shares[None, :, None]).astype(jnp.bfloat16)

    def place_rows(rows_in, where_to):
        return jnp.zeros((E * CAP, DW), jnp.bfloat16).at[where_to].set(rows_in)

    def arm_major(sent):
        return sent.reshape(N_DP, N_EXPERT, E, CAP, DW).transpose(2, 0, 1, 3, 4).reshape(E, N_DP, N_EXPERT * CAP, DW)

    def block_major(done):
        return done.reshape(E, N_DP, N_EXPERT, CAP, DW).transpose(1, 2, 0, 3, 4).reshape(block_count, E * CAP, DW)

    sent_tokens = arm_major(jax.vmap(place_rows)(token_rows, destination))
    sent_cot = arm_major(jax.vmap(place_rows)(cot_rows, destination))
    out_rows, input_rows, grad_gate, grad_up, grad_down = lax.map(arm_pass, (sent_tokens, sent_cot, w_gate, w_up, w_down))

    def pick_rows(table, where_to):
        return table[where_to]

    back_out = jax.vmap(pick_rows)(block_major(out_rows), destination).reshape(TOKENS, 2, DW).astype(jnp.float32)
    back_input = jax.vmap(pick_rows)(block_major(input_rows), destination).reshape(TOKENS, 2, DW).astype(jnp.float32)
    head_output = (fact_share * back_out[:, 0] + counter_share * back_out[:, 1]).astype(jnp.bfloat16)
    grad_tokens = (back_input[:, 0] + back_input[:, 1]).astype(jnp.bfloat16)
    return (head_output, grad_tokens, grad_gate, grad_up, grad_down)
```

```python
import functools

import jax
import jax.numpy as jnp
from jax import lax
from jax.experimental import pallas as pl
from jax.experimental.pallas import tpu as pltpu
from jax.sharding import PartitionSpec as P

fact_share = 0.7
counter_share = 0.3
MESH_ID = pl.DeviceIdType.MESH


def silu_parts(gate_pre):
    sigmoid_gate = jax.nn.sigmoid(gate_pre)
    return (gate_pre * sigmoid_gate, sigmoid_gate * (1.0 + gate_pre * (1.0 - sigmoid_gate)))


def exchange_kernel(n, send_hbm, recv_hbm, send_sem, recv_sem, local_sem):
    me = lax.axis_index("expert")
    row = lax.axis_index("dp")

    def copy_to(i):
        j = lax.rem(me + i, n)
        return pltpu.make_async_remote_copy(
            src_ref=send_hbm.at[j],
            dst_ref=recv_hbm.at[me],
            send_sem=send_sem.at[j],
            recv_sem=recv_sem.at[me],
            device_id=(row, j),
            device_id_type=MESH_ID,
        )

    def start(i, carry):
        copy_to(i).start()
        return carry

    lax.fori_loop(1, n, start, 0)
    local = pltpu.make_async_copy(send_hbm.at[me], recv_hbm.at[me], local_sem)
    local.start()
    local.wait()

    def finish(i, carry):
        j = lax.rem(me + i, n)
        copy_to(i).wait_send()
        pltpu.make_async_remote_copy(
            src_ref=send_hbm.at[j],
            dst_ref=recv_hbm.at[j],
            send_sem=send_sem.at[j],
            recv_sem=recv_sem.at[j],
            device_id=(row, j),
            device_id_type=MESH_ID,
        ).wait_recv()
        return carry

    lax.fori_loop(1, n, finish, 0)


def exchange(send):
    n = send.shape[0]
    nbytes = send.size * send.dtype.itemsize
    return pl.pallas_call(
        functools.partial(exchange_kernel, n),
        out_shape=jax.ShapeDtypeStruct(send.shape, send.dtype),
        in_specs=[pl.BlockSpec(memory_space=pl.ANY)],
        out_specs=pl.BlockSpec(memory_space=pl.ANY),
        scratch_shapes=[
            pltpu.SemaphoreType.DMA((n,)),
            pltpu.SemaphoreType.DMA((n,)),
            pltpu.SemaphoreType.DMA,
        ],
        compiler_params=pltpu.CompilerParams(has_side_effects=True),
        cost_estimate=pl.CostEstimate(flops=0, bytes_accessed=2 * nbytes, transcendentals=0),
    )(send)


def on_device(tokens, codes, cotangent, w_gate, w_up, w_down):
    token_count, feature_width = tokens.shape
    local_arms = w_gate.shape[0]
    arm_count = local_arms * lax.axis_size("expert")
    capacity = 4 * token_count // arm_count
    flat_codes = codes.reshape(-1)
    arm_ids = jnp.arange(arm_count, dtype=jnp.int32)
    onehot = (flat_codes[:, None] == arm_ids[None, :]).astype(jnp.int32)
    earlier = jnp.cumsum(onehot, axis=0) - onehot
    slot = jnp.sum(earlier * onehot, axis=1)
    tok_dest = flat_codes * (2 * capacity) + slot
    cot_dest = tok_dest + capacity
    shares = jnp.tile(jnp.array([fact_share, counter_share], jnp.float32), token_count)
    token_rows = jnp.repeat(tokens, 2, axis=0)
    cot_rows = (jnp.repeat(cotangent.astype(jnp.float32), 2, axis=0) * shares[:, None]).astype(
        jnp.bfloat16
    )
    send = (
        jnp.zeros((arm_count * 2 * capacity, feature_width), jnp.bfloat16)
        .at[jnp.concatenate([tok_dest, cot_dest])]
        .set(jnp.concatenate([token_rows, cot_rows]))
        .reshape(arm_count, 2 * capacity, feature_width)
    )
    got = exchange(send)
    arm_tokens = got[:, :capacity].reshape(1, -1, feature_width)
    arm_cot = got[:, capacity:].reshape(1, -1, feature_width)

    gate_pre = jnp.einsum("arc,ach->arh", arm_tokens, w_gate, preferred_element_type=jnp.float32)
    up_pre = jnp.einsum("arc,ach->arh", arm_tokens, w_up, preferred_element_type=jnp.float32)
    activated, silu_slope = silu_parts(gate_pre)
    hidden = (activated * up_pre).astype(jnp.bfloat16)
    out_rows = jnp.einsum(
        "arh,ahc->arc", hidden, w_down, preferred_element_type=jnp.float32
    ).astype(jnp.bfloat16)
    d_hidden = jnp.einsum("arc,ahc->arh", arm_cot, w_down, preferred_element_type=jnp.float32)
    d_up = (d_hidden * activated).astype(jnp.bfloat16)
    d_gate = (d_hidden * up_pre * silu_slope).astype(jnp.bfloat16)
    input_rows = (
        jnp.einsum("arh,ach->arc", d_gate, w_gate, preferred_element_type=jnp.float32)
        + jnp.einsum("arh,ach->arc", d_up, w_up, preferred_element_type=jnp.float32)
    ).astype(jnp.bfloat16)

    ret = jnp.concatenate(
        [
            out_rows.reshape(-1, capacity, feature_width),
            input_rows.reshape(-1, capacity, feature_width),
        ],
        axis=1,
    )
    back = exchange(ret).reshape(arm_count * 2 * capacity, feature_width)
    back_out = back[tok_dest].reshape(token_count, 2, feature_width).astype(jnp.float32)
    back_input = back[cot_dest].reshape(token_count, 2, feature_width).astype(jnp.float32)
    head_output = (fact_share * back_out[:, 0] + counter_share * back_out[:, 1]).astype(
        jnp.bfloat16
    )
    grad_tokens = (back_input[:, 0] + back_input[:, 1]).astype(jnp.bfloat16)

    partial_gate = jnp.einsum(
        "arc,arh->ach", arm_tokens, d_gate, preferred_element_type=jnp.float32
    )
    partial_up = jnp.einsum("arc,arh->ach", arm_tokens, d_up, preferred_element_type=jnp.float32)
    partial_down = jnp.einsum("arh,arc->ahc", hidden, arm_cot, preferred_element_type=jnp.float32)
    summed_gate, summed_up, summed_down = (
        lax.psum_scatter(
            partial_gate.astype(jnp.bfloat16), "dp", scatter_dimension=2, tiled=True
        ).astype(jnp.float32),
        lax.psum_scatter(
            partial_up.astype(jnp.bfloat16), "dp", scatter_dimension=2, tiled=True
        ).astype(jnp.float32),
        lax.psum_scatter(
            partial_down.astype(jnp.bfloat16), "dp", scatter_dimension=1, tiled=True
        ).astype(jnp.float32),
    )
    grad_gate = summed_gate.astype(jnp.bfloat16)
    grad_up = summed_up.astype(jnp.bfloat16)
    grad_down = summed_down.astype(jnp.bfloat16)
    return (head_output, grad_tokens, grad_gate, grad_up, grad_down)


def solution(mesh):
    return jax.shard_map(
        on_device,
        mesh=mesh,
        in_specs=(
            P(("dp", "expert"), None),
            P(("dp", "expert"), None),
            P(("dp", "expert"), None),
            P("expert", None, None),
            P("expert", None, None),
            P("expert", None, None),
        ),
        out_specs=(
            P(("dp", "expert"), None),
            P(("dp", "expert"), None),
            P("expert", None, "dp"),
            P("expert", None, "dp"),
            P("expert", "dp", None),
        ),
        check_vma=False,
    )
```

```python
import functools

import jax
import jax.numpy as jnp
from jax import lax
from jax.experimental import pallas as pl
from jax.experimental.pallas import tpu as pltpu
from jax.sharding import PartitionSpec as P

fact_share = 0.7
counter_share = 0.3
MESH_ID = pl.DeviceIdType.MESH


def silu_parts(gate_pre):
    sigmoid_gate = jax.nn.sigmoid(gate_pre)
    return (gate_pre * sigmoid_gate, sigmoid_gate * (1.0 + gate_pre * (1.0 - sigmoid_gate)))


def exchange_kernel(n, send_hbm, recv_hbm, send_sem, recv_sem, local_sem):
    me = lax.axis_index("expert")
    row = lax.axis_index("dp")

    def copy_to(i):
        j = lax.rem(me + i, n)
        return pltpu.make_async_remote_copy(
            src_ref=send_hbm.at[j],
            dst_ref=recv_hbm.at[me],
            send_sem=send_sem.at[j],
            recv_sem=recv_sem.at[me],
            device_id=(row, j),
            device_id_type=MESH_ID,
        )

    def start(i, carry):
        copy_to(i).start()
        return carry

    lax.fori_loop(1, n, start, 0)
    local = pltpu.make_async_copy(send_hbm.at[me], recv_hbm.at[me], local_sem)
    local.start()
    local.wait()

    def finish(i, carry):
        j = lax.rem(me + i, n)
        copy_to(i).wait_send()
        pltpu.make_async_remote_copy(
            src_ref=send_hbm.at[j],
            dst_ref=recv_hbm.at[j],
            send_sem=send_sem.at[j],
            recv_sem=recv_sem.at[j],
            device_id=(row, j),
            device_id_type=MESH_ID,
        ).wait_recv()
        return carry

    lax.fori_loop(1, n, finish, 0)


def exchange(send):
    n = send.shape[0]
    nbytes = send.size * send.dtype.itemsize
    return pl.pallas_call(
        functools.partial(exchange_kernel, n),
        out_shape=jax.ShapeDtypeStruct(send.shape, send.dtype),
        in_specs=[pl.BlockSpec(memory_space=pl.ANY)],
        out_specs=pl.BlockSpec(memory_space=pl.ANY),
        scratch_shapes=[
            pltpu.SemaphoreType.DMA((n,)),
            pltpu.SemaphoreType.DMA((n,)),
            pltpu.SemaphoreType.DMA,
        ],
        compiler_params=pltpu.CompilerParams(has_side_effects=True),
        cost_estimate=pl.CostEstimate(flops=0, bytes_accessed=2 * nbytes, transcendentals=0),
    )(send)


def on_device(tokens, codes, cotangent, w_gate, w_up, w_down):
    token_count, feature_width = tokens.shape
    local_arms = w_gate.shape[0]
    arm_count = local_arms * lax.axis_size("expert")
    capacity = 4 * token_count // arm_count
    flat_codes = codes.reshape(-1)
    arm_ids = jnp.arange(arm_count, dtype=jnp.int32)
    onehot = (flat_codes[:, None] == arm_ids[None, :]).astype(jnp.int32)
    earlier = jnp.cumsum(onehot, axis=0) - onehot
    slot = jnp.sum(earlier * onehot, axis=1)
    tok_dest = flat_codes * (2 * capacity) + slot
    cot_dest = tok_dest + capacity
    shares = jnp.tile(jnp.array([fact_share, counter_share], jnp.float32), token_count)
    token_rows = jnp.repeat(tokens, 2, axis=0)
    cot_rows = (jnp.repeat(cotangent.astype(jnp.float32), 2, axis=0) * shares[:, None]).astype(
        jnp.bfloat16
    )
    send = (
        jnp.zeros((arm_count * 2 * capacity, feature_width), jnp.bfloat16)
        .at[jnp.concatenate([tok_dest, cot_dest])]
        .set(jnp.concatenate([token_rows, cot_rows]))
        .reshape(arm_count, 2 * capacity, feature_width)
    )
    got = lax.all_to_all(send, "expert", 0, 0, tiled=True)
    arm_tokens = got[:, :capacity].reshape(1, -1, feature_width)
    arm_cot = got[:, capacity:].reshape(1, -1, feature_width)

    gate_pre = jnp.einsum("arc,ach->arh", arm_tokens, w_gate, preferred_element_type=jnp.float32)
    up_pre = jnp.einsum("arc,ach->arh", arm_tokens, w_up, preferred_element_type=jnp.float32)
    activated, silu_slope = silu_parts(gate_pre)
    hidden = (activated * up_pre).astype(jnp.bfloat16)
    out_rows = jnp.einsum(
        "arh,ahc->arc", hidden, w_down, preferred_element_type=jnp.float32
    ).astype(jnp.bfloat16)
    d_hidden = jnp.einsum("arc,ahc->arh", arm_cot, w_down, preferred_element_type=jnp.float32)
    d_up = (d_hidden * activated).astype(jnp.bfloat16)
    d_gate = (d_hidden * up_pre * silu_slope).astype(jnp.bfloat16)
    input_rows = (
        jnp.einsum("arh,ach->arc", d_gate, w_gate, preferred_element_type=jnp.float32)
        + jnp.einsum("arh,ach->arc", d_up, w_up, preferred_element_type=jnp.float32)
    ).astype(jnp.bfloat16)

    ret = jnp.concatenate(
        [
            out_rows.reshape(-1, capacity, feature_width),
            input_rows.reshape(-1, capacity, feature_width),
        ],
        axis=1,
    )
    back = lax.all_to_all(ret, "expert", 0, 0, tiled=True).reshape(arm_count * 2 * capacity, feature_width)
    back_out = back[tok_dest].reshape(token_count, 2, feature_width).astype(jnp.float32)
    back_input = back[cot_dest].reshape(token_count, 2, feature_width).astype(jnp.float32)
    head_output = (fact_share * back_out[:, 0] + counter_share * back_out[:, 1]).astype(
        jnp.bfloat16
    )
    grad_tokens = (back_input[:, 0] + back_input[:, 1]).astype(jnp.bfloat16)

    partials = jnp.stack(
        [
            jnp.einsum("arh,arc->hc", d_gate, arm_tokens, preferred_element_type=jnp.float32),
            jnp.einsum("arh,arc->hc", d_up, arm_tokens, preferred_element_type=jnp.float32),
            jnp.einsum("arh,arc->hc", hidden, arm_cot, preferred_element_type=jnp.float32),
        ],
        axis=1,
    ).astype(jnp.bfloat16)
    summed = lax.psum_scatter(partials, "dp", scatter_dimension=0, tiled=True)
    grad_gate = summed[:, 0, :].T[None]
    grad_up = summed[:, 1, :].T[None]
    grad_down = summed[:, 2, :][None]
    return (head_output, grad_tokens, grad_gate, grad_up, grad_down)


def solution(mesh):
    return jax.shard_map(
        on_device,
        mesh=mesh,
        in_specs=(
            P(("dp", "expert"), None),
            P(("dp", "expert"), None),
            P(("dp", "expert"), None),
            P("expert", None, None),
            P("expert", None, None),
            P("expert", None, None),
        ),
        out_specs=(
            P(("dp", "expert"), None),
            P(("dp", "expert"), None),
            P("expert", None, "dp"),
            P("expert", None, "dp"),
            P("expert", "dp", None),
        ),
        check_vma=False,
    )
```

```python
import functools

import jax
import jax.numpy as jnp
from jax import lax
from jax.experimental import pallas as pl
from jax.experimental.pallas import tpu as pltpu
from jax.sharding import PartitionSpec as P

fact_share = 0.7
counter_share = 0.3
MESH_ID = pl.DeviceIdType.MESH


def silu_parts(gate_pre):
    sigmoid_gate = jax.nn.sigmoid(gate_pre)
    return (gate_pre * sigmoid_gate, sigmoid_gate * (1.0 + gate_pre * (1.0 - sigmoid_gate)))


def exchange_kernel(n, send_hbm, recv_hbm, send_sem, recv_sem, local_sem):
    me = lax.axis_index("expert")
    row = lax.axis_index("dp")

    def copy_to(i):
        j = lax.rem(me + i, n)
        return pltpu.make_async_remote_copy(
            src_ref=send_hbm.at[j],
            dst_ref=recv_hbm.at[me],
            send_sem=send_sem.at[j],
            recv_sem=recv_sem.at[me],
            device_id=(row, j),
            device_id_type=MESH_ID,
        )

    def start(i, carry):
        copy_to(i).start()
        return carry

    lax.fori_loop(1, n, start, 0)
    local = pltpu.make_async_copy(send_hbm.at[me], recv_hbm.at[me], local_sem)
    local.start()
    local.wait()

    def finish(i, carry):
        j = lax.rem(me + i, n)
        copy_to(i).wait_send()
        pltpu.make_async_remote_copy(
            src_ref=send_hbm.at[j],
            dst_ref=recv_hbm.at[j],
            send_sem=send_sem.at[j],
            recv_sem=recv_sem.at[j],
            device_id=(row, j),
            device_id_type=MESH_ID,
        ).wait_recv()
        return carry

    lax.fori_loop(1, n, finish, 0)


def exchange(send):
    n = send.shape[0]
    nbytes = send.size * send.dtype.itemsize
    return pl.pallas_call(
        functools.partial(exchange_kernel, n),
        out_shape=jax.ShapeDtypeStruct(send.shape, send.dtype),
        in_specs=[pl.BlockSpec(memory_space=pl.ANY)],
        out_specs=pl.BlockSpec(memory_space=pl.ANY),
        scratch_shapes=[
            pltpu.SemaphoreType.DMA((n,)),
            pltpu.SemaphoreType.DMA((n,)),
            pltpu.SemaphoreType.DMA,
        ],
        compiler_params=pltpu.CompilerParams(has_side_effects=True),
        cost_estimate=pl.CostEstimate(flops=0, bytes_accessed=2 * nbytes, transcendentals=0),
    )(send)


def contract_rows(a, b):
    return lax.dot_general(a, b, (((0,), (0,)), ((), ())), preferred_element_type=jnp.float32)


def contract_cols(a, b):
    return lax.dot_general(a, b, (((1,), (1,)), ((), ())), preferred_element_type=jnp.float32)


def arm_kernel(tok_ref, cot_ref, wg_ref, wu_ref, wd_ref, out_ref, inp_ref, gu_ref, down_ref, acc_g, acc_u, acc_d):
    step = pl.program_id(0)
    hidden_width = wg_ref.shape[1]

    @pl.when(step == 0)
    def _():
        acc_g[...] = jnp.zeros_like(acc_g)
        acc_u[...] = jnp.zeros_like(acc_u)
        acc_d[...] = jnp.zeros_like(acc_d)

    x = tok_ref[...]
    c = cot_ref[...]
    wg = wg_ref[...]
    wu = wu_ref[...]
    wd = wd_ref[...]
    gate_pre = jnp.dot(x, wg, preferred_element_type=jnp.float32)
    up_pre = jnp.dot(x, wu, preferred_element_type=jnp.float32)
    activated, silu_slope = silu_parts(gate_pre)
    hidden = (activated * up_pre).astype(jnp.bfloat16)
    out_ref[...] = jnp.dot(hidden, wd, preferred_element_type=jnp.float32).astype(out_ref.dtype)
    d_hidden = contract_cols(c, wd)
    d_up = (d_hidden * activated).astype(jnp.bfloat16)
    d_gate = (d_hidden * up_pre * silu_slope).astype(jnp.bfloat16)
    inp_ref[...] = (contract_cols(d_gate, wg) + contract_cols(d_up, wu)).astype(inp_ref.dtype)
    acc_g[...] += contract_rows(x, d_gate)
    acc_u[...] += contract_rows(x, d_up)
    acc_d[...] += contract_rows(hidden, c)

    @pl.when(step == pl.num_programs(0) - 1)
    def _():
        gu_ref[:, :hidden_width] = acc_g[...].astype(gu_ref.dtype)
        gu_ref[:, hidden_width:] = acc_u[...].astype(gu_ref.dtype)
        down_ref[...] = acc_d[...].astype(down_ref.dtype)


def arm_math(tokens, cot, wg, wu, wd):
    rows, width = tokens.shape
    hidden_width = wg.shape[1]
    block = 128
    row_spec = pl.BlockSpec((block, width), lambda i: (i, 0))
    whole = lambda shape: pl.BlockSpec(shape, lambda i: (0, 0))
    flops = 2 * rows * width * hidden_width * 9
    return pl.pallas_call(
        arm_kernel,
        grid=(rows // block,),
        in_specs=[row_spec, row_spec, whole(wg.shape), whole(wu.shape), whole(wd.shape)],
        out_specs=[row_spec, row_spec, whole((width, 2 * hidden_width)), whole((hidden_width, width))],
        out_shape=[
            jax.ShapeDtypeStruct((rows, width), jnp.bfloat16),
            jax.ShapeDtypeStruct((rows, width), jnp.bfloat16),
            jax.ShapeDtypeStruct((width, 2 * hidden_width), jnp.bfloat16),
            jax.ShapeDtypeStruct((hidden_width, width), jnp.bfloat16),
        ],
        scratch_shapes=[
            pltpu.VMEM((width, hidden_width), jnp.float32),
            pltpu.VMEM((width, hidden_width), jnp.float32),
            pltpu.VMEM((hidden_width, width), jnp.float32),
        ],
        compiler_params=pltpu.CompilerParams(
            dimension_semantics=("arbitrary",), vmem_limit_bytes=48 * 1024 * 1024
        ),
        cost_estimate=pl.CostEstimate(
            flops=flops, bytes_accessed=2 * (4 * rows * width + 6 * width * hidden_width), transcendentals=rows * hidden_width
        ),
    )(tokens, cot, wg, wu, wd)


def on_device(tokens, codes, cotangent, w_gate, w_up, w_down):
    token_count, feature_width = tokens.shape
    local_arms = w_gate.shape[0]
    arm_count = local_arms * lax.axis_size("expert")
    capacity = 4 * token_count // arm_count
    flat_codes = codes.reshape(-1)
    arm_ids = jnp.arange(arm_count, dtype=jnp.int32)
    onehot = (flat_codes[:, None] == arm_ids[None, :]).astype(jnp.int32)
    earlier = jnp.cumsum(onehot, axis=0) - onehot
    slot = jnp.sum(earlier * onehot, axis=1)
    tok_dest = flat_codes * (2 * capacity) + slot
    cot_dest = tok_dest + capacity
    shares = jnp.tile(jnp.array([fact_share, counter_share], jnp.float32), token_count)
    token_rows = jnp.repeat(tokens, 2, axis=0)
    cot_rows = (jnp.repeat(cotangent.astype(jnp.float32), 2, axis=0) * shares[:, None]).astype(
        jnp.bfloat16
    )
    send = (
        jnp.zeros((arm_count * 2 * capacity, feature_width), jnp.bfloat16)
        .at[jnp.concatenate([tok_dest, cot_dest])]
        .set(jnp.concatenate([token_rows, cot_rows]))
        .reshape(arm_count, 2 * capacity, feature_width)
    )
    got = lax.all_to_all(send, "expert", 0, 0, tiled=True)
    arm_tokens = got[:, :capacity].reshape(1, -1, feature_width)
    arm_cot = got[:, capacity:].reshape(1, -1, feature_width)

    out_rows, input_rows, part_gu, part_down = arm_math(
        arm_tokens[0], arm_cot[0], w_gate[0], w_up[0], w_down[0]
    )
    ret = jnp.concatenate(
        [
            out_rows.reshape(-1, capacity, feature_width),
            input_rows.reshape(-1, capacity, feature_width),
        ],
        axis=1,
    )
    back = lax.all_to_all(ret, "expert", 0, 0, tiled=True).reshape(arm_count * 2 * capacity, feature_width)
    back_out = back[tok_dest].reshape(token_count, 2, feature_width).astype(jnp.float32)
    back_input = back[cot_dest].reshape(token_count, 2, feature_width).astype(jnp.float32)
    head_output = (fact_share * back_out[:, 0] + counter_share * back_out[:, 1]).astype(
        jnp.bfloat16
    )
    grad_tokens = (back_input[:, 0] + back_input[:, 1]).astype(jnp.bfloat16)

    hidden_width = w_gate.shape[2]
    summed_gu = lax.psum_scatter(
        part_gu.reshape(feature_width, 2, hidden_width), "dp", scatter_dimension=2, tiled=True
    )
    summed_down = lax.psum_scatter(part_down, "dp", scatter_dimension=0, tiled=True)
    grad_gate = summed_gu[None, :, 0, :]
    grad_up = summed_gu[None, :, 1, :]
    grad_down = summed_down[None]
    return (head_output, grad_tokens, grad_gate, grad_up, grad_down)


def solution(mesh):
    return jax.shard_map(
        on_device,
        mesh=mesh,
        in_specs=(
            P(("dp", "expert"), None),
            P(("dp", "expert"), None),
            P(("dp", "expert"), None),
            P("expert", None, None),
            P("expert", None, None),
            P("expert", None, None),
        ),
        out_specs=(
            P(("dp", "expert"), None),
            P(("dp", "expert"), None),
            P("expert", None, "dp"),
            P("expert", None, "dp"),
            P("expert", "dp", None),
        ),
        check_vma=False,
    )
```

```python
import functools

import jax
import jax.numpy as jnp
from jax import lax
from jax.experimental import pallas as pl
from jax.experimental.pallas import tpu as pltpu
from jax.sharding import PartitionSpec as P

fact_share = 0.7
counter_share = 0.3
MESH_ID = pl.DeviceIdType.MESH


def silu_parts(gate_pre):
    sigmoid_gate = jax.nn.sigmoid(gate_pre)
    return (gate_pre * sigmoid_gate, sigmoid_gate * (1.0 + gate_pre * (1.0 - sigmoid_gate)))


def exchange_kernel(n, send_hbm, recv_hbm, send_sem, recv_sem, local_sem):
    me = lax.axis_index("expert")
    row = lax.axis_index("dp")

    def copy_to(i):
        j = lax.rem(me + i, n)
        return pltpu.make_async_remote_copy(
            src_ref=send_hbm.at[j],
            dst_ref=recv_hbm.at[me],
            send_sem=send_sem.at[j],
            recv_sem=recv_sem.at[me],
            device_id=(row, j),
            device_id_type=MESH_ID,
        )

    def start(i, carry):
        copy_to(i).start()
        return carry

    lax.fori_loop(1, n, start, 0)
    local = pltpu.make_async_copy(send_hbm.at[me], recv_hbm.at[me], local_sem)
    local.start()
    local.wait()

    def finish(i, carry):
        j = lax.rem(me + i, n)
        copy_to(i).wait_send()
        pltpu.make_async_remote_copy(
            src_ref=send_hbm.at[j],
            dst_ref=recv_hbm.at[j],
            send_sem=send_sem.at[j],
            recv_sem=recv_sem.at[j],
            device_id=(row, j),
            device_id_type=MESH_ID,
        ).wait_recv()
        return carry

    lax.fori_loop(1, n, finish, 0)


def exchange(send):
    n = send.shape[0]
    nbytes = send.size * send.dtype.itemsize
    return pl.pallas_call(
        functools.partial(exchange_kernel, n),
        out_shape=jax.ShapeDtypeStruct(send.shape, send.dtype),
        in_specs=[pl.BlockSpec(memory_space=pl.ANY)],
        out_specs=pl.BlockSpec(memory_space=pl.ANY),
        scratch_shapes=[
            pltpu.SemaphoreType.DMA((n,)),
            pltpu.SemaphoreType.DMA((n,)),
            pltpu.SemaphoreType.DMA,
        ],
        compiler_params=pltpu.CompilerParams(has_side_effects=True),
        cost_estimate=pl.CostEstimate(flops=0, bytes_accessed=2 * nbytes, transcendentals=0),
    )(send)


def contract_rows(a, b):
    return lax.dot_general(a, b, (((0,), (0,)), ((), ())), preferred_element_type=jnp.float32)


def contract_cols(a, b):
    return lax.dot_general(a, b, (((1,), (1,)), ((), ())), preferred_element_type=jnp.float32)


def arm_kernel(tok_ref, cot_ref, wg_ref, wu_ref, wd_ref, out_ref, inp_ref, part_ref, acc_g, acc_u, acc_d):
    step = pl.program_id(0)
    hidden_width = wg_ref.shape[1]

    @pl.when(step == 0)
    def _():
        acc_g[...] = jnp.zeros_like(acc_g)
        acc_u[...] = jnp.zeros_like(acc_u)
        acc_d[...] = jnp.zeros_like(acc_d)

    x = tok_ref[...]
    c = cot_ref[...]
    wg = wg_ref[...]
    wu = wu_ref[...]
    wd = wd_ref[...]
    gate_pre = jnp.dot(x, wg, preferred_element_type=jnp.float32)
    up_pre = jnp.dot(x, wu, preferred_element_type=jnp.float32)
    activated, silu_slope = silu_parts(gate_pre)
    hidden = (activated * up_pre).astype(jnp.bfloat16)
    out_ref[...] = jnp.dot(hidden, wd, preferred_element_type=jnp.float32).astype(out_ref.dtype)
    d_hidden = contract_cols(c, wd)
    d_up = (d_hidden * activated).astype(jnp.bfloat16)
    d_gate = (d_hidden * up_pre * silu_slope).astype(jnp.bfloat16)
    inp_ref[...] = (contract_cols(d_gate, wg) + contract_cols(d_up, wu)).astype(inp_ref.dtype)
    acc_g[...] += contract_rows(x, d_gate)
    acc_u[...] += contract_rows(x, d_up)
    acc_d[...] += contract_rows(c, hidden)

    @pl.when(step == pl.num_programs(0) - 1)
    def _():
        part_ref[0] = acc_g[...].astype(part_ref.dtype)
        part_ref[1] = acc_u[...].astype(part_ref.dtype)
        part_ref[2] = acc_d[...].astype(part_ref.dtype)


def arm_math(tokens, cot, wg, wu, wd):
    rows, width = tokens.shape
    hidden_width = wg.shape[1]
    block = 256
    row_spec = pl.BlockSpec((block, width), lambda i: (i, 0))
    whole = lambda shape: pl.BlockSpec(shape, lambda i: (0, 0))
    flops = 2 * rows * width * hidden_width * 9
    return pl.pallas_call(
        arm_kernel,
        grid=(rows // block,),
        in_specs=[row_spec, row_spec, whole(wg.shape), whole(wu.shape), whole(wd.shape)],
        out_specs=[
            row_spec,
            row_spec,
            pl.BlockSpec((3, width, hidden_width), lambda i: (0, 0, 0)),
        ],
        out_shape=[
            jax.ShapeDtypeStruct((rows, width), jnp.bfloat16),
            jax.ShapeDtypeStruct((rows, width), jnp.bfloat16),
            jax.ShapeDtypeStruct((3, width, hidden_width), jnp.bfloat16),
        ],
        scratch_shapes=[
            pltpu.VMEM((width, hidden_width), jnp.float32),
            pltpu.VMEM((width, hidden_width), jnp.float32),
            pltpu.VMEM((width, hidden_width), jnp.float32),
        ],
        compiler_params=pltpu.CompilerParams(
            dimension_semantics=("arbitrary",), vmem_limit_bytes=48 * 1024 * 1024
        ),
        cost_estimate=pl.CostEstimate(
            flops=flops, bytes_accessed=2 * (4 * rows * width + 6 * width * hidden_width), transcendentals=rows * hidden_width
        ),
    )(tokens, cot, wg, wu, wd)


def on_device(tokens, codes, cotangent, w_gate, w_up, w_down):
    token_count, feature_width = tokens.shape
    local_arms = w_gate.shape[0]
    arm_count = local_arms * lax.axis_size("expert")
    capacity = 4 * token_count // arm_count
    flat_codes = codes.reshape(-1)
    arm_ids = jnp.arange(arm_count, dtype=jnp.int32)
    onehot = (flat_codes[:, None] == arm_ids[None, :]).astype(jnp.int32)
    earlier = jnp.cumsum(onehot, axis=0) - onehot
    slot = jnp.sum(earlier * onehot, axis=1)
    tok_dest = flat_codes * (2 * capacity) + slot
    cot_dest = tok_dest + capacity
    shares = jnp.tile(jnp.array([fact_share, counter_share], jnp.float32), token_count)
    token_rows = jnp.repeat(tokens, 2, axis=0)
    cot_rows = (jnp.repeat(cotangent.astype(jnp.float32), 2, axis=0) * shares[:, None]).astype(
        jnp.bfloat16
    )
    send = (
        jnp.zeros((arm_count * 2 * capacity, feature_width), jnp.bfloat16)
        .at[jnp.concatenate([tok_dest, cot_dest])]
        .set(jnp.concatenate([token_rows, cot_rows]))
        .reshape(arm_count, 2 * capacity, feature_width)
    )
    got = lax.all_to_all(send, "expert", 0, 0, tiled=True)
    arm_tokens = got[:, :capacity].reshape(1, -1, feature_width)
    arm_cot = got[:, capacity:].reshape(1, -1, feature_width)

    out_rows, input_rows, partials = arm_math(
        arm_tokens[0], arm_cot[0], w_gate[0], w_up[0], w_down[0]
    )
    ret = jnp.concatenate(
        [
            out_rows.reshape(-1, capacity, feature_width),
            input_rows.reshape(-1, capacity, feature_width),
        ],
        axis=1,
    )
    back = lax.all_to_all(ret, "expert", 0, 0, tiled=True).reshape(arm_count * 2 * capacity, feature_width)
    back_out = back[tok_dest].reshape(token_count, 2, feature_width).astype(jnp.float32)
    back_input = back[cot_dest].reshape(token_count, 2, feature_width).astype(jnp.float32)
    head_output = (fact_share * back_out[:, 0] + counter_share * back_out[:, 1]).astype(
        jnp.bfloat16
    )
    grad_tokens = (back_input[:, 0] + back_input[:, 1]).astype(jnp.bfloat16)

    summed = lax.psum_scatter(partials, "dp", scatter_dimension=2, tiled=True)
    grad_gate = summed[0:1]
    grad_up = summed[1:2]
    grad_down = summed[2].T[None]
    return (head_output, grad_tokens, grad_gate, grad_up, grad_down)


def solution(mesh):
    return jax.shard_map(
        on_device,
        mesh=mesh,
        in_specs=(
            P(("dp", "expert"), None),
            P(("dp", "expert"), None),
            P(("dp", "expert"), None),
            P("expert", None, None),
            P("expert", None, None),
            P("expert", None, None),
        ),
        out_specs=(
            P(("dp", "expert"), None),
            P(("dp", "expert"), None),
            P("expert", None, "dp"),
            P("expert", None, "dp"),
            P("expert", "dp", None),
        ),
        check_vma=False,
    )
```

```python
import functools

import jax
import jax.numpy as jnp
from jax import lax
from jax.experimental import pallas as pl
from jax.experimental.pallas import tpu as pltpu
from jax.sharding import PartitionSpec as P

fact_share = 0.7
counter_share = 0.3
MESH_ID = pl.DeviceIdType.MESH


def silu_parts(gate_pre):
    sigmoid_gate = jax.nn.sigmoid(gate_pre)
    return (gate_pre * sigmoid_gate, sigmoid_gate * (1.0 + gate_pre * (1.0 - sigmoid_gate)))


def exchange_kernel(n, send_hbm, recv_hbm, send_sem, recv_sem, local_sem):
    me = lax.axis_index("expert")
    row = lax.axis_index("dp")

    def copy_to(i):
        j = lax.rem(me + i, n)
        return pltpu.make_async_remote_copy(
            src_ref=send_hbm.at[j],
            dst_ref=recv_hbm.at[me],
            send_sem=send_sem.at[j],
            recv_sem=recv_sem.at[me],
            device_id=(row, j),
            device_id_type=MESH_ID,
        )

    def start(i, carry):
        copy_to(i).start()
        return carry

    lax.fori_loop(1, n, start, 0)
    local = pltpu.make_async_copy(send_hbm.at[me], recv_hbm.at[me], local_sem)
    local.start()
    local.wait()

    def finish(i, carry):
        j = lax.rem(me + i, n)
        copy_to(i).wait_send()
        pltpu.make_async_remote_copy(
            src_ref=send_hbm.at[j],
            dst_ref=recv_hbm.at[j],
            send_sem=send_sem.at[j],
            recv_sem=recv_sem.at[j],
            device_id=(row, j),
            device_id_type=MESH_ID,
        ).wait_recv()
        return carry

    lax.fori_loop(1, n, finish, 0)


def exchange(send):
    n = send.shape[0]
    nbytes = send.size * send.dtype.itemsize
    return pl.pallas_call(
        functools.partial(exchange_kernel, n),
        out_shape=jax.ShapeDtypeStruct(send.shape, send.dtype),
        in_specs=[pl.BlockSpec(memory_space=pl.ANY)],
        out_specs=pl.BlockSpec(memory_space=pl.ANY),
        scratch_shapes=[
            pltpu.SemaphoreType.DMA((n,)),
            pltpu.SemaphoreType.DMA((n,)),
            pltpu.SemaphoreType.DMA,
        ],
        compiler_params=pltpu.CompilerParams(has_side_effects=True),
        cost_estimate=pl.CostEstimate(flops=0, bytes_accessed=2 * nbytes, transcendentals=0),
    )(send)


def contract_rows(a, b):
    return lax.dot_general(a, b, (((0,), (0,)), ((), ())), preferred_element_type=jnp.float32)


def contract_cols(a, b):
    return lax.dot_general(a, b, (((1,), (1,)), ((), ())), preferred_element_type=jnp.float32)


def arm_kernel(
    tok_ref, cot_ref, wg_hbm, wu_hbm, wd_hbm, out_ref, inp_ref, part_ref,
    wg_ref, wu_ref, wd_ref, acc_g, acc_u, acc_d, sems,
):
    step = pl.program_id(0)
    hidden_width = wg_ref.shape[1]
    loads = [
        pltpu.make_async_copy(src, dst, sems.at[k])
        for k, (src, dst) in enumerate(((wg_hbm, wg_ref), (wu_hbm, wu_ref), (wd_hbm, wd_ref)))
    ]

    @pl.when(step == 0)
    def _():
        for load in loads:
            load.start()
        acc_g[...] = jnp.zeros_like(acc_g)
        acc_u[...] = jnp.zeros_like(acc_u)
        acc_d[...] = jnp.zeros_like(acc_d)
        loads[0].wait()
        loads[1].wait()

    x = tok_ref[...]
    c = cot_ref[...]
    wg = wg_ref[...]
    wu = wu_ref[...]
    gate_pre = jnp.dot(x, wg, preferred_element_type=jnp.float32)
    up_pre = jnp.dot(x, wu, preferred_element_type=jnp.float32)
    activated, silu_slope = silu_parts(gate_pre)
    hidden = (activated * up_pre).astype(jnp.bfloat16)

    @pl.when(step == 0)
    def _():
        loads[2].wait()

    wd = wd_ref[...]
    out_ref[...] = jnp.dot(hidden, wd, preferred_element_type=jnp.float32).astype(out_ref.dtype)
    d_hidden = contract_cols(c, wd)
    d_up = (d_hidden * activated).astype(jnp.bfloat16)
    d_gate = (d_hidden * up_pre * silu_slope).astype(jnp.bfloat16)
    inp_ref[...] = (contract_cols(d_gate, wg) + contract_cols(d_up, wu)).astype(inp_ref.dtype)
    acc_g[...] += contract_rows(x, d_gate)
    acc_u[...] += contract_rows(x, d_up)
    acc_d[...] += contract_rows(c, hidden)

    @pl.when(step == pl.num_programs(0) - 1)
    def _():
        part_ref[0] = acc_g[...].astype(part_ref.dtype)
        part_ref[1] = acc_u[...].astype(part_ref.dtype)
        part_ref[2] = acc_d[...].astype(part_ref.dtype)


def arm_math(tokens, cot, wg, wu, wd):
    rows, width = tokens.shape
    hidden_width = wg.shape[1]
    block = 256
    row_spec = pl.BlockSpec((block, width), lambda i: (i, 0))
    flops = 2 * rows * width * hidden_width * 9
    return pl.pallas_call(
        arm_kernel,
        grid=(rows // block,),
        in_specs=[row_spec, row_spec] + [pl.BlockSpec(memory_space=pl.ANY)] * 3,
        out_specs=[
            row_spec,
            row_spec,
            pl.BlockSpec((3, width, hidden_width), lambda i: (0, 0, 0)),
        ],
        out_shape=[
            jax.ShapeDtypeStruct((rows, width), jnp.bfloat16),
            jax.ShapeDtypeStruct((rows, width), jnp.bfloat16),
            jax.ShapeDtypeStruct((3, width, hidden_width), jnp.bfloat16),
        ],
        scratch_shapes=[
            pltpu.VMEM(wg.shape, wg.dtype),
            pltpu.VMEM(wu.shape, wu.dtype),
            pltpu.VMEM(wd.shape, wd.dtype),
            pltpu.VMEM((width, hidden_width), jnp.float32),
            pltpu.VMEM((width, hidden_width), jnp.float32),
            pltpu.VMEM((width, hidden_width), jnp.float32),
            pltpu.SemaphoreType.DMA((3,)),
        ],
        compiler_params=pltpu.CompilerParams(
            dimension_semantics=("arbitrary",), vmem_limit_bytes=48 * 1024 * 1024
        ),
        cost_estimate=pl.CostEstimate(
            flops=flops, bytes_accessed=2 * (4 * rows * width + 6 * width * hidden_width), transcendentals=rows * hidden_width
        ),
    )(tokens, cot, wg, wu, wd)


def on_device(tokens, codes, cotangent, w_gate, w_up, w_down):
    token_count, feature_width = tokens.shape
    local_arms = w_gate.shape[0]
    arm_count = local_arms * lax.axis_size("expert")
    capacity = 4 * token_count // arm_count
    flat_codes = codes.reshape(-1)
    arm_ids = jnp.arange(arm_count, dtype=jnp.int32)
    onehot = (flat_codes[:, None] == arm_ids[None, :]).astype(jnp.int32)
    earlier = jnp.cumsum(onehot, axis=0) - onehot
    slot = jnp.sum(earlier * onehot, axis=1)
    tok_dest = flat_codes * (2 * capacity) + slot
    cot_dest = tok_dest + capacity
    shares = jnp.tile(jnp.array([fact_share, counter_share], jnp.float32), token_count)
    token_rows = jnp.repeat(tokens, 2, axis=0)
    cot_rows = (jnp.repeat(cotangent.astype(jnp.float32), 2, axis=0) * shares[:, None]).astype(
        jnp.bfloat16
    )
    send = (
        jnp.zeros((arm_count * 2 * capacity, feature_width), jnp.bfloat16)
        .at[jnp.concatenate([tok_dest, cot_dest])]
        .set(jnp.concatenate([token_rows, cot_rows]))
        .reshape(arm_count, 2 * capacity, feature_width)
    )
    got = lax.all_to_all(send, "expert", 0, 0, tiled=True)
    arm_tokens = got[:, :capacity].reshape(1, -1, feature_width)
    arm_cot = got[:, capacity:].reshape(1, -1, feature_width)

    out_rows, input_rows, partials = arm_math(
        arm_tokens[0], arm_cot[0], w_gate[0], w_up[0], w_down[0]
    )
    ret = jnp.concatenate(
        [
            out_rows.reshape(-1, capacity, feature_width),
            input_rows.reshape(-1, capacity, feature_width),
        ],
        axis=1,
    )
    back = lax.all_to_all(ret, "expert", 0, 0, tiled=True).reshape(arm_count * 2 * capacity, feature_width)
    back_out = back[tok_dest].reshape(token_count, 2, feature_width).astype(jnp.float32)
    back_input = back[cot_dest].reshape(token_count, 2, feature_width).astype(jnp.float32)
    head_output = (fact_share * back_out[:, 0] + counter_share * back_out[:, 1]).astype(
        jnp.bfloat16
    )
    grad_tokens = (back_input[:, 0] + back_input[:, 1]).astype(jnp.bfloat16)

    summed = lax.psum_scatter(partials, "dp", scatter_dimension=2, tiled=True)
    grad_gate = summed[0:1]
    grad_up = summed[1:2]
    grad_down = summed[2].T[None]
    return (head_output, grad_tokens, grad_gate, grad_up, grad_down)


def solution(mesh):
    return jax.shard_map(
        on_device,
        mesh=mesh,
        in_specs=(
            P(("dp", "expert"), None),
            P(("dp", "expert"), None),
            P(("dp", "expert"), None),
            P("expert", None, None),
            P("expert", None, None),
            P("expert", None, None),
        ),
        out_specs=(
            P(("dp", "expert"), None),
            P(("dp", "expert"), None),
            P("expert", None, "dp"),
            P("expert", None, "dp"),
            P("expert", "dp", None),
        ),
        check_vma=False,
    )
```

```python
import functools

import jax
import jax.numpy as jnp
from jax import lax
from jax.experimental import pallas as pl
from jax.experimental.pallas import tpu as pltpu
from jax.sharding import PartitionSpec as P

fact_share = 0.7
counter_share = 0.3
MESH_ID = pl.DeviceIdType.MESH


def silu_parts(gate_pre):
    sigmoid_gate = jax.nn.sigmoid(gate_pre)
    return (gate_pre * sigmoid_gate, sigmoid_gate * (1.0 + gate_pre * (1.0 - sigmoid_gate)))


def exchange_kernel(n, send_hbm, recv_hbm, send_sem, recv_sem, local_sem):
    me = lax.axis_index("expert")
    row = lax.axis_index("dp")

    def copy_to(i):
        j = lax.rem(me + i, n)
        return pltpu.make_async_remote_copy(
            src_ref=send_hbm.at[j],
            dst_ref=recv_hbm.at[me],
            send_sem=send_sem.at[j],
            recv_sem=recv_sem.at[me],
            device_id=(row, j),
            device_id_type=MESH_ID,
        )

    def start(i, carry):
        copy_to(i).start()
        return carry

    lax.fori_loop(1, n, start, 0)
    local = pltpu.make_async_copy(send_hbm.at[me], recv_hbm.at[me], local_sem)
    local.start()
    local.wait()

    def finish(i, carry):
        j = lax.rem(me + i, n)
        copy_to(i).wait_send()
        pltpu.make_async_remote_copy(
            src_ref=send_hbm.at[j],
            dst_ref=recv_hbm.at[j],
            send_sem=send_sem.at[j],
            recv_sem=recv_sem.at[j],
            device_id=(row, j),
            device_id_type=MESH_ID,
        ).wait_recv()
        return carry

    lax.fori_loop(1, n, finish, 0)


def exchange(send):
    n = send.shape[0]
    nbytes = send.size * send.dtype.itemsize
    return pl.pallas_call(
        functools.partial(exchange_kernel, n),
        out_shape=jax.ShapeDtypeStruct(send.shape, send.dtype),
        in_specs=[pl.BlockSpec(memory_space=pl.ANY)],
        out_specs=pl.BlockSpec(memory_space=pl.ANY),
        scratch_shapes=[
            pltpu.SemaphoreType.DMA((n,)),
            pltpu.SemaphoreType.DMA((n,)),
            pltpu.SemaphoreType.DMA,
        ],
        compiler_params=pltpu.CompilerParams(has_side_effects=True),
        cost_estimate=pl.CostEstimate(flops=0, bytes_accessed=2 * nbytes, transcendentals=0),
    )(send)


def contract_rows(a, b):
    return lax.dot_general(a, b, (((0,), (0,)), ((), ())), preferred_element_type=jnp.float32)


def contract_cols(a, b):
    return lax.dot_general(a, b, (((1,), (1,)), ((), ())), preferred_element_type=jnp.float32)


def arm_kernel(
    tok_ref, cot_ref, wg_hbm, wu_hbm, wd_hbm, out_ref, inp_ref, part_ref,
    wg_ref, wu_ref, wd_ref, acc_g, acc_u, acc_d, sems,
):
    step = pl.program_id(0)
    hidden_width = wg_ref.shape[1]
    loads = [
        pltpu.make_async_copy(src, dst, sems.at[k])
        for k, (src, dst) in enumerate(((wg_hbm, wg_ref), (wu_hbm, wu_ref), (wd_hbm, wd_ref)))
    ]

    @pl.when(step == 0)
    def _():
        for load in loads:
            load.start()
        acc_g[...] = jnp.zeros_like(acc_g)
        acc_u[...] = jnp.zeros_like(acc_u)
        acc_d[...] = jnp.zeros_like(acc_d)
        loads[0].wait()
        loads[1].wait()

    x = tok_ref[...]
    c = cot_ref[...]
    wg = wg_ref[...]
    wu = wu_ref[...]
    gate_pre = jnp.dot(x, wg, preferred_element_type=jnp.float32)
    up_pre = jnp.dot(x, wu, preferred_element_type=jnp.float32)
    activated, silu_slope = silu_parts(gate_pre)
    hidden = (activated * up_pre).astype(jnp.bfloat16)

    @pl.when(step == 0)
    def _():
        loads[2].wait()

    wd = wd_ref[...]
    out_ref[...] = jnp.dot(hidden, wd, preferred_element_type=jnp.float32).astype(out_ref.dtype)
    d_hidden = contract_cols(c, wd)
    d_up = (d_hidden * activated).astype(jnp.bfloat16)
    d_gate = (d_hidden * up_pre * silu_slope).astype(jnp.bfloat16)
    inp_ref[...] = (contract_cols(d_gate, wg) + contract_cols(d_up, wu)).astype(inp_ref.dtype)
    acc_g[...] += contract_rows(x, d_gate)
    acc_u[...] += contract_rows(x, d_up)
    acc_d[...] += contract_rows(c, hidden)

    @pl.when(step == pl.num_programs(0) - 1)
    def _():
        part_ref[0] = acc_g[...].astype(part_ref.dtype)
        part_ref[1] = acc_u[...].astype(part_ref.dtype)
        part_ref[2] = acc_d[...].astype(part_ref.dtype)


def arm_math(tokens, cot, wg, wu, wd):
    rows, width = tokens.shape
    hidden_width = wg.shape[1]
    block = 256
    row_spec = pl.BlockSpec((block, width), lambda i: (i, 0))
    flops = 2 * rows * width * hidden_width * 9
    return pl.pallas_call(
        arm_kernel,
        grid=(rows // block,),
        in_specs=[row_spec, row_spec] + [pl.BlockSpec(memory_space=pltpu.HBM)] * 3,
        out_specs=[
            row_spec,
            row_spec,
            pl.BlockSpec((3, width, hidden_width), lambda i: (0, 0, 0)),
        ],
        out_shape=[
            jax.ShapeDtypeStruct((rows, width), jnp.bfloat16),
            jax.ShapeDtypeStruct((rows, width), jnp.bfloat16),
            jax.ShapeDtypeStruct((3, width, hidden_width), jnp.bfloat16),
        ],
        scratch_shapes=[
            pltpu.VMEM(wg.shape, wg.dtype),
            pltpu.VMEM(wu.shape, wu.dtype),
            pltpu.VMEM(wd.shape, wd.dtype),
            pltpu.VMEM((width, hidden_width), jnp.float32),
            pltpu.VMEM((width, hidden_width), jnp.float32),
            pltpu.VMEM((width, hidden_width), jnp.float32),
            pltpu.SemaphoreType.DMA((3,)),
        ],
        compiler_params=pltpu.CompilerParams(
            dimension_semantics=("arbitrary",), vmem_limit_bytes=67043328
        ),
        cost_estimate=pl.CostEstimate(
            flops=flops, bytes_accessed=2 * (4 * rows * width + 6 * width * hidden_width), transcendentals=rows * hidden_width
        ),
    )(tokens, cot, wg, wu, wd)


def on_device(tokens, codes, cotangent, w_gate, w_up, w_down):
    token_count, feature_width = tokens.shape
    local_arms = w_gate.shape[0]
    arm_count = local_arms * lax.axis_size("expert")
    capacity = 4 * token_count // arm_count
    flat_codes = codes.reshape(-1)
    arm_ids = jnp.arange(arm_count, dtype=jnp.int32)
    onehot = (flat_codes[:, None] == arm_ids[None, :]).astype(jnp.int32)
    earlier = jnp.cumsum(onehot, axis=0) - onehot
    slot = jnp.sum(earlier * onehot, axis=1)
    tok_dest = flat_codes * (2 * capacity) + slot
    cot_dest = tok_dest + capacity
    shares = jnp.tile(jnp.array([fact_share, counter_share], jnp.float32), token_count)
    token_rows = jnp.repeat(tokens, 2, axis=0)
    cot_rows = (jnp.repeat(cotangent.astype(jnp.float32), 2, axis=0) * shares[:, None]).astype(
        jnp.bfloat16
    )
    send = (
        jnp.zeros((arm_count * 2 * capacity, feature_width), jnp.bfloat16)
        .at[jnp.concatenate([tok_dest, cot_dest])]
        .set(jnp.concatenate([token_rows, cot_rows]))
        .reshape(arm_count, 2 * capacity, feature_width)
    )
    got = lax.all_to_all(send, "expert", 0, 0, tiled=True)
    arm_tokens = got[:, :capacity].reshape(1, -1, feature_width)
    arm_cot = got[:, capacity:].reshape(1, -1, feature_width)

    out_rows, input_rows, partials = arm_math(
        arm_tokens[0], arm_cot[0], w_gate[0], w_up[0], w_down[0]
    )
    ret = jnp.concatenate(
        [
            out_rows.reshape(-1, capacity, feature_width),
            input_rows.reshape(-1, capacity, feature_width),
        ],
        axis=1,
    )
    back = lax.all_to_all(ret, "expert", 0, 0, tiled=True).reshape(arm_count * 2 * capacity, feature_width)
    back_out = back[tok_dest].reshape(token_count, 2, feature_width).astype(jnp.float32)
    back_input = back[cot_dest].reshape(token_count, 2, feature_width).astype(jnp.float32)
    head_output = (fact_share * back_out[:, 0] + counter_share * back_out[:, 1]).astype(
        jnp.bfloat16
    )
    grad_tokens = (back_input[:, 0] + back_input[:, 1]).astype(jnp.bfloat16)

    summed = lax.psum_scatter(partials, "dp", scatter_dimension=2, tiled=True)
    grad_gate = summed[0:1]
    grad_up = summed[1:2]
    grad_down = summed[2].T[None]
    return (head_output, grad_tokens, grad_gate, grad_up, grad_down)


def solution(mesh):
    return jax.shard_map(
        on_device,
        mesh=mesh,
        in_specs=(
            P(("dp", "expert"), None),
            P(("dp", "expert"), None),
            P(("dp", "expert"), None),
            P("expert", None, None),
            P("expert", None, None),
            P("expert", None, None),
        ),
        out_specs=(
            P(("dp", "expert"), None),
            P(("dp", "expert"), None),
            P("expert", None, "dp"),
            P("expert", None, "dp"),
            P("expert", "dp", None),
        ),
        check_vma=False,
    )
```

```python
import functools

import jax
import jax.numpy as jnp
from jax import lax
from jax.experimental import pallas as pl
from jax.experimental.pallas import tpu as pltpu
from jax.sharding import PartitionSpec as P

fact_share = 0.7
counter_share = 0.3
MESH_ID = pl.DeviceIdType.MESH


def silu_parts(gate_pre):
    sigmoid_gate = jax.nn.sigmoid(gate_pre)
    return (gate_pre * sigmoid_gate, sigmoid_gate * (1.0 + gate_pre * (1.0 - sigmoid_gate)))


def exchange_kernel(n, send_hbm, recv_hbm, send_sem, recv_sem, local_sem):
    me = lax.axis_index("expert")
    row = lax.axis_index("dp")

    def copy_to(i):
        j = lax.rem(me + i, n)
        return pltpu.make_async_remote_copy(
            src_ref=send_hbm.at[j],
            dst_ref=recv_hbm.at[me],
            send_sem=send_sem.at[j],
            recv_sem=recv_sem.at[me],
            device_id=(row, j),
            device_id_type=MESH_ID,
        )

    def start(i, carry):
        copy_to(i).start()
        return carry

    lax.fori_loop(1, n, start, 0)
    local = pltpu.make_async_copy(send_hbm.at[me], recv_hbm.at[me], local_sem)
    local.start()
    local.wait()

    def finish(i, carry):
        j = lax.rem(me + i, n)
        copy_to(i).wait_send()
        pltpu.make_async_remote_copy(
            src_ref=send_hbm.at[j],
            dst_ref=recv_hbm.at[j],
            send_sem=send_sem.at[j],
            recv_sem=recv_sem.at[j],
            device_id=(row, j),
            device_id_type=MESH_ID,
        ).wait_recv()
        return carry

    lax.fori_loop(1, n, finish, 0)


def exchange(send):
    n = send.shape[0]
    nbytes = send.size * send.dtype.itemsize
    return pl.pallas_call(
        functools.partial(exchange_kernel, n),
        out_shape=jax.ShapeDtypeStruct(send.shape, send.dtype),
        in_specs=[pl.BlockSpec(memory_space=pl.ANY)],
        out_specs=pl.BlockSpec(memory_space=pl.ANY),
        scratch_shapes=[
            pltpu.SemaphoreType.DMA((n,)),
            pltpu.SemaphoreType.DMA((n,)),
            pltpu.SemaphoreType.DMA,
        ],
        compiler_params=pltpu.CompilerParams(has_side_effects=True),
        cost_estimate=pl.CostEstimate(flops=0, bytes_accessed=2 * nbytes, transcendentals=0),
    )(send)


def contract_rows(a, b):
    return lax.dot_general(a, b, (((0,), (0,)), ((), ())), preferred_element_type=jnp.float32)


def contract_cols(a, b):
    return lax.dot_general(a, b, (((1,), (1,)), ((), ())), preferred_element_type=jnp.float32)


def arm_kernel(tok_ref, cot_ref, wg_ref, wu_ref, wd_ref, out_ref, inp_ref, part_ref, acc_g, acc_u, acc_d):
    step = pl.program_id(0)
    hidden_width = wg_ref.shape[1]

    @pl.when(step == 0)
    def _():
        acc_g[...] = jnp.zeros_like(acc_g)
        acc_u[...] = jnp.zeros_like(acc_u)
        acc_d[...] = jnp.zeros_like(acc_d)

    x = tok_ref[...]
    c = cot_ref[...]
    wg = wg_ref[...]
    wu = wu_ref[...]
    wd = wd_ref[...]
    gate_pre = jnp.dot(x, wg, preferred_element_type=jnp.float32)
    up_pre = jnp.dot(x, wu, preferred_element_type=jnp.float32)
    activated, silu_slope = silu_parts(gate_pre)
    hidden = (activated * up_pre).astype(jnp.bfloat16)
    out_ref[...] = jnp.dot(hidden, wd, preferred_element_type=jnp.float32).astype(out_ref.dtype)
    d_hidden = contract_cols(c, wd)
    d_up = (d_hidden * activated).astype(jnp.bfloat16)
    d_gate = (d_hidden * up_pre * silu_slope).astype(jnp.bfloat16)
    inp_ref[...] = (contract_cols(d_gate, wg) + contract_cols(d_up, wu)).astype(inp_ref.dtype)
    acc_g[...] += contract_rows(x, d_gate)
    acc_u[...] += contract_rows(x, d_up)
    acc_d[...] += contract_rows(c, hidden)

    @pl.when(step == pl.num_programs(0) - 1)
    def _():
        part_ref[0] = acc_g[...].astype(part_ref.dtype)
        part_ref[1] = acc_u[...].astype(part_ref.dtype)
        part_ref[2] = acc_d[...].astype(part_ref.dtype)


def arm_math(tokens, cot, wg, wu, wd):
    rows, width = tokens.shape
    hidden_width = wg.shape[1]
    block = 256
    row_spec = pl.BlockSpec((block, width), lambda i: (i, 0))
    whole = lambda shape: pl.BlockSpec(shape, lambda i: (0, 0))
    flops = 2 * rows * width * hidden_width * 9
    return pl.pallas_call(
        arm_kernel,
        grid=(rows // block,),
        in_specs=[row_spec, row_spec, whole(wg.shape), whole(wu.shape), whole(wd.shape)],
        out_specs=[
            row_spec,
            row_spec,
            pl.BlockSpec((3, width, hidden_width), lambda i: (0, 0, 0)),
        ],
        out_shape=[
            jax.ShapeDtypeStruct((rows, width), jnp.bfloat16),
            jax.ShapeDtypeStruct((rows, width), jnp.bfloat16),
            jax.ShapeDtypeStruct((3, width, hidden_width), jnp.bfloat16),
        ],
        scratch_shapes=[
            pltpu.VMEM((width, hidden_width), jnp.float32),
            pltpu.VMEM((width, hidden_width), jnp.float32),
            pltpu.VMEM((width, hidden_width), jnp.float32),
        ],
        compiler_params=pltpu.CompilerParams(
            dimension_semantics=("arbitrary",), vmem_limit_bytes=48 * 1024 * 1024
        ),
        cost_estimate=pl.CostEstimate(
            flops=flops, bytes_accessed=2 * (4 * rows * width + 6 * width * hidden_width), transcendentals=rows * hidden_width
        ),
    )(tokens, cot, wg, wu, wd)


def on_device(tokens, codes, cotangent, w_gate, w_up, w_down):
    token_count, feature_width = tokens.shape
    local_arms = w_gate.shape[0]
    arm_count = local_arms * lax.axis_size("expert")
    capacity = 4 * token_count // arm_count
    flat_codes = codes.reshape(-1)
    arm_ids = jnp.arange(arm_count, dtype=jnp.int32)
    onehot = (flat_codes[:, None] == arm_ids[None, :]).astype(jnp.int32)
    earlier = jnp.cumsum(onehot, axis=0) - onehot
    slot = jnp.sum(earlier * onehot, axis=1)
    tok_dest = flat_codes * (2 * capacity) + slot
    cot_dest = tok_dest + capacity
    cot_f = cotangent.astype(jnp.float32)
    sources = jnp.concatenate(
        [tokens, tokens, (cot_f * fact_share).astype(jnp.bfloat16), (cot_f * counter_share).astype(jnp.bfloat16)]
    )
    dest = jnp.concatenate([tok_dest[0::2], tok_dest[1::2], cot_dest[0::2], cot_dest[1::2]])
    place = (
        lax.broadcasted_iota(jnp.int32, (arm_count * 2 * capacity, dest.shape[0]), 0) == dest[None, :]
    ).astype(jnp.bfloat16)
    send = (
        jnp.dot(place, sources, preferred_element_type=jnp.float32)
        .astype(jnp.bfloat16)
        .reshape(arm_count, 2 * capacity, feature_width)
    )
    got = lax.all_to_all(send, "expert", 0, 0, tiled=True)
    arm_tokens = got[:, :capacity].reshape(1, -1, feature_width)
    arm_cot = got[:, capacity:].reshape(1, -1, feature_width)

    out_rows, input_rows, partials = arm_math(
        arm_tokens[0], arm_cot[0], w_gate[0], w_up[0], w_down[0]
    )
    ret = jnp.concatenate(
        [
            out_rows.reshape(-1, capacity, feature_width),
            input_rows.reshape(-1, capacity, feature_width),
        ],
        axis=1,
    )
    back = lax.all_to_all(ret, "expert", 0, 0, tiled=True).reshape(-1, feature_width)
    picked = lax.dot_general(
        place, back, (((0,), (0,)), ((), ())), preferred_element_type=jnp.float32
    ).reshape(4, token_count, feature_width)
    head_output = (fact_share * picked[0] + counter_share * picked[1]).astype(jnp.bfloat16)
    grad_tokens = (picked[2] + picked[3]).astype(jnp.bfloat16)

    summed = lax.psum_scatter(partials, "dp", scatter_dimension=2, tiled=True)
    grad_gate = summed[0:1]
    grad_up = summed[1:2]
    grad_down = summed[2].T[None]
    return (head_output, grad_tokens, grad_gate, grad_up, grad_down)


def solution(mesh):
    return jax.shard_map(
        on_device,
        mesh=mesh,
        in_specs=(
            P(("dp", "expert"), None),
            P(("dp", "expert"), None),
            P(("dp", "expert"), None),
            P("expert", None, None),
            P("expert", None, None),
            P("expert", None, None),
        ),
        out_specs=(
            P(("dp", "expert"), None),
            P(("dp", "expert"), None),
            P("expert", None, "dp"),
            P("expert", None, "dp"),
            P("expert", "dp", None),
        ),
        check_vma=False,
    )
```

```python
import functools

import jax
import jax.numpy as jnp
from jax import lax
from jax.experimental import pallas as pl
from jax.experimental.pallas import tpu as pltpu
from jax.sharding import PartitionSpec as P

fact_share = 0.7
counter_share = 0.3
MESH_ID = pl.DeviceIdType.MESH


def silu_parts(gate_pre):
    sigmoid_gate = jax.nn.sigmoid(gate_pre)
    return (gate_pre * sigmoid_gate, sigmoid_gate * (1.0 + gate_pre * (1.0 - sigmoid_gate)))


def exchange_kernel(n, send_hbm, recv_hbm, send_sem, recv_sem, local_sem):
    me = lax.axis_index("expert")
    row = lax.axis_index("dp")

    def copy_to(i):
        j = lax.rem(me + i, n)
        return pltpu.make_async_remote_copy(
            src_ref=send_hbm.at[j],
            dst_ref=recv_hbm.at[me],
            send_sem=send_sem.at[j],
            recv_sem=recv_sem.at[me],
            device_id=(row, j),
            device_id_type=MESH_ID,
        )

    def start(i, carry):
        copy_to(i).start()
        return carry

    lax.fori_loop(1, n, start, 0)
    local = pltpu.make_async_copy(send_hbm.at[me], recv_hbm.at[me], local_sem)
    local.start()
    local.wait()

    def finish(i, carry):
        j = lax.rem(me + i, n)
        copy_to(i).wait_send()
        pltpu.make_async_remote_copy(
            src_ref=send_hbm.at[j],
            dst_ref=recv_hbm.at[j],
            send_sem=send_sem.at[j],
            recv_sem=recv_sem.at[j],
            device_id=(row, j),
            device_id_type=MESH_ID,
        ).wait_recv()
        return carry

    lax.fori_loop(1, n, finish, 0)


def exchange(send):
    n = send.shape[0]
    nbytes = send.size * send.dtype.itemsize
    return pl.pallas_call(
        functools.partial(exchange_kernel, n),
        out_shape=jax.ShapeDtypeStruct(send.shape, send.dtype),
        in_specs=[pl.BlockSpec(memory_space=pl.ANY)],
        out_specs=pl.BlockSpec(memory_space=pl.ANY),
        scratch_shapes=[
            pltpu.SemaphoreType.DMA((n,)),
            pltpu.SemaphoreType.DMA((n,)),
            pltpu.SemaphoreType.DMA,
        ],
        compiler_params=pltpu.CompilerParams(has_side_effects=True),
        cost_estimate=pl.CostEstimate(flops=0, bytes_accessed=2 * nbytes, transcendentals=0),
    )(send)


def contract_rows(a, b):
    return lax.dot_general(a, b, (((0,), (0,)), ((), ())), preferred_element_type=jnp.float32)


def contract_cols(a, b):
    return lax.dot_general(a, b, (((1,), (1,)), ((), ())), preferred_element_type=jnp.float32)


def arm_kernel(tok_ref, cot_ref, wg_ref, wu_ref, wd_ref, out_ref, inp_ref, part_ref, acc_g, acc_u, acc_d):
    step = pl.program_id(0)
    hidden_width = wg_ref.shape[1]

    @pl.when(step == 0)
    def _():
        acc_g[...] = jnp.zeros_like(acc_g)
        acc_u[...] = jnp.zeros_like(acc_u)
        acc_d[...] = jnp.zeros_like(acc_d)

    x = tok_ref[...]
    c = cot_ref[...]
    wg = wg_ref[...]
    wu = wu_ref[...]
    wd = wd_ref[...]
    gate_pre = jnp.dot(x, wg, preferred_element_type=jnp.float32)
    up_pre = jnp.dot(x, wu, preferred_element_type=jnp.float32)
    activated, silu_slope = silu_parts(gate_pre)
    hidden = (activated * up_pre).astype(jnp.bfloat16)
    out_ref[...] = jnp.dot(hidden, wd, preferred_element_type=jnp.float32).astype(out_ref.dtype)
    d_hidden = contract_cols(c, wd)
    d_up = (d_hidden * activated).astype(jnp.bfloat16)
    d_gate = (d_hidden * up_pre * silu_slope).astype(jnp.bfloat16)
    inp_ref[...] = (contract_cols(d_gate, wg) + contract_cols(d_up, wu)).astype(inp_ref.dtype)
    acc_g[...] += contract_rows(x, d_gate)
    acc_u[...] += contract_rows(x, d_up)
    acc_d[...] += contract_rows(c, hidden)

    @pl.when(step == pl.num_programs(0) - 1)
    def _():
        part_ref[0] = acc_g[...].astype(part_ref.dtype)
        part_ref[1] = acc_u[...].astype(part_ref.dtype)
        part_ref[2] = acc_d[...].astype(part_ref.dtype)


def arm_math(tokens, cot, wg, wu, wd):
    rows, width = tokens.shape
    hidden_width = wg.shape[1]
    block = 512
    row_spec = pl.BlockSpec((block, width), lambda i: (i, 0))
    whole = lambda shape: pl.BlockSpec(shape, lambda i: (0, 0))
    flops = 2 * rows * width * hidden_width * 9
    return pl.pallas_call(
        arm_kernel,
        grid=(rows // block,),
        in_specs=[row_spec, row_spec, whole(wg.shape), whole(wu.shape), whole(wd.shape)],
        out_specs=[
            row_spec,
            row_spec,
            pl.BlockSpec((3, width, hidden_width), lambda i: (0, 0, 0)),
        ],
        out_shape=[
            jax.ShapeDtypeStruct((rows, width), jnp.bfloat16),
            jax.ShapeDtypeStruct((rows, width), jnp.bfloat16),
            jax.ShapeDtypeStruct((3, width, hidden_width), jnp.bfloat16),
        ],
        scratch_shapes=[
            pltpu.VMEM((width, hidden_width), jnp.float32),
            pltpu.VMEM((width, hidden_width), jnp.float32),
            pltpu.VMEM((width, hidden_width), jnp.float32),
        ],
        compiler_params=pltpu.CompilerParams(
            dimension_semantics=("arbitrary",), vmem_limit_bytes=48 * 1024 * 1024
        ),
        cost_estimate=pl.CostEstimate(
            flops=flops, bytes_accessed=2 * (4 * rows * width + 6 * width * hidden_width), transcendentals=rows * hidden_width
        ),
    )(tokens, cot, wg, wu, wd)


def on_device(tokens, codes, cotangent, w_gate, w_up, w_down):
    token_count, feature_width = tokens.shape
    local_arms = w_gate.shape[0]
    arm_count = local_arms * lax.axis_size("expert")
    capacity = 4 * token_count // arm_count
    flat_codes = codes.reshape(-1)
    arm_ids = jnp.arange(arm_count, dtype=jnp.int32)
    onehot = (flat_codes[:, None] == arm_ids[None, :]).astype(jnp.int32)
    earlier = jnp.cumsum(onehot, axis=0) - onehot
    slot = jnp.sum(earlier * onehot, axis=1)
    tok_dest = flat_codes * (2 * capacity) + slot
    cot_dest = tok_dest + capacity
    cot_f = cotangent.astype(jnp.float32)
    sources = jnp.concatenate(
        [tokens, tokens, (cot_f * fact_share).astype(jnp.bfloat16), (cot_f * counter_share).astype(jnp.bfloat16)]
    )
    dest = jnp.concatenate([tok_dest[0::2], tok_dest[1::2], cot_dest[0::2], cot_dest[1::2]])
    place = (
        lax.broadcasted_iota(jnp.int32, (arm_count * 2 * capacity, dest.shape[0]), 0) == dest[None, :]
    ).astype(jnp.bfloat16)
    send = (
        jnp.dot(place, sources, preferred_element_type=jnp.float32)
        .astype(jnp.bfloat16)
        .reshape(arm_count, 2 * capacity, feature_width)
    )
    got = lax.all_to_all(send, "expert", 0, 0, tiled=True)
    arm_tokens = got[:, :capacity].reshape(1, -1, feature_width)
    arm_cot = got[:, capacity:].reshape(1, -1, feature_width)

    out_rows, input_rows, partials = arm_math(
        arm_tokens[0], arm_cot[0], w_gate[0], w_up[0], w_down[0]
    )
    ret = jnp.concatenate(
        [
            out_rows.reshape(-1, capacity, feature_width),
            input_rows.reshape(-1, capacity, feature_width),
        ],
        axis=1,
    )
    back = lax.all_to_all(ret, "expert", 0, 0, tiled=True).reshape(-1, feature_width)
    picked = lax.dot_general(
        place, back, (((0,), (0,)), ((), ())), preferred_element_type=jnp.float32
    ).reshape(4, token_count, feature_width)
    head_output = (fact_share * picked[0] + counter_share * picked[1]).astype(jnp.bfloat16)
    grad_tokens = (picked[2] + picked[3]).astype(jnp.bfloat16)

    summed = lax.psum_scatter(partials, "dp", scatter_dimension=2, tiled=True)
    grad_gate = summed[0:1]
    grad_up = summed[1:2]
    grad_down = summed[2].T[None]
    return (head_output, grad_tokens, grad_gate, grad_up, grad_down)


def solution(mesh):
    return jax.shard_map(
        on_device,
        mesh=mesh,
        in_specs=(
            P(("dp", "expert"), None),
            P(("dp", "expert"), None),
            P(("dp", "expert"), None),
            P("expert", None, None),
            P("expert", None, None),
            P("expert", None, None),
        ),
        out_specs=(
            P(("dp", "expert"), None),
            P(("dp", "expert"), None),
            P("expert", None, "dp"),
            P("expert", None, "dp"),
            P("expert", "dp", None),
        ),
        check_vma=False,
    )
```

```python
import functools

import jax
import jax.numpy as jnp
from jax import lax
from jax.experimental import pallas as pl
from jax.experimental.pallas import tpu as pltpu
from jax.sharding import PartitionSpec as P

fact_share = 0.7
counter_share = 0.3
MESH_ID = pl.DeviceIdType.MESH


def silu_parts(gate_pre):
    sigmoid_gate = jax.nn.sigmoid(gate_pre)
    return (gate_pre * sigmoid_gate, sigmoid_gate * (1.0 + gate_pre * (1.0 - sigmoid_gate)))


def exchange_kernel(n, send_hbm, recv_hbm, send_sem, recv_sem, local_sem):
    me = lax.axis_index("expert")
    row = lax.axis_index("dp")

    def copy_to(i):
        j = lax.rem(me + i, n)
        return pltpu.make_async_remote_copy(
            src_ref=send_hbm.at[j],
            dst_ref=recv_hbm.at[me],
            send_sem=send_sem.at[j],
            recv_sem=recv_sem.at[me],
            device_id=(row, j),
            device_id_type=MESH_ID,
        )

    def start(i, carry):
        copy_to(i).start()
        return carry

    lax.fori_loop(1, n, start, 0)
    local = pltpu.make_async_copy(send_hbm.at[me], recv_hbm.at[me], local_sem)
    local.start()
    local.wait()

    def finish(i, carry):
        j = lax.rem(me + i, n)
        copy_to(i).wait_send()
        pltpu.make_async_remote_copy(
            src_ref=send_hbm.at[j],
            dst_ref=recv_hbm.at[j],
            send_sem=send_sem.at[j],
            recv_sem=recv_sem.at[j],
            device_id=(row, j),
            device_id_type=MESH_ID,
        ).wait_recv()
        return carry

    lax.fori_loop(1, n, finish, 0)


def exchange(send):
    n = send.shape[0]
    nbytes = send.size * send.dtype.itemsize
    return pl.pallas_call(
        functools.partial(exchange_kernel, n),
        out_shape=jax.ShapeDtypeStruct(send.shape, send.dtype),
        in_specs=[pl.BlockSpec(memory_space=pl.ANY)],
        out_specs=pl.BlockSpec(memory_space=pl.ANY),
        scratch_shapes=[
            pltpu.SemaphoreType.DMA((n,)),
            pltpu.SemaphoreType.DMA((n,)),
            pltpu.SemaphoreType.DMA,
        ],
        compiler_params=pltpu.CompilerParams(has_side_effects=True),
        cost_estimate=pl.CostEstimate(flops=0, bytes_accessed=2 * nbytes, transcendentals=0),
    )(send)


def contract_rows(a, b):
    return lax.dot_general(a, b, (((0,), (0,)), ((), ())), preferred_element_type=jnp.float32)


def contract_cols(a, b):
    return lax.dot_general(a, b, (((1,), (1,)), ((), ())), preferred_element_type=jnp.float32)


def arm_kernel(tok_ref, cot_ref, wg_ref, wu_ref, wd_ref, out_ref, inp_ref, part_ref, acc_g, acc_u, acc_d):
    step = pl.program_id(0)
    hidden_width = wg_ref.shape[1]

    @pl.when(step == 0)
    def _():
        acc_g[...] = jnp.zeros_like(acc_g)
        acc_u[...] = jnp.zeros_like(acc_u)
        acc_d[...] = jnp.zeros_like(acc_d)

    x = tok_ref[...]
    c = cot_ref[...]
    wg = wg_ref[...]
    wu = wu_ref[...]
    wd = wd_ref[...]
    gate_pre = jnp.dot(x, wg, preferred_element_type=jnp.float32)
    up_pre = jnp.dot(x, wu, preferred_element_type=jnp.float32)
    activated, silu_slope = silu_parts(gate_pre)
    hidden = (activated * up_pre).astype(jnp.bfloat16)
    out_ref[...] = jnp.dot(hidden, wd, preferred_element_type=jnp.float32).astype(out_ref.dtype)
    d_hidden = contract_cols(c, wd)
    d_up = (d_hidden * activated).astype(jnp.bfloat16)
    d_gate = (d_hidden * up_pre * silu_slope).astype(jnp.bfloat16)
    inp_ref[...] = (contract_cols(d_gate, wg) + contract_cols(d_up, wu)).astype(inp_ref.dtype)
    acc_g[...] += contract_rows(x, d_gate)
    acc_u[...] += contract_rows(x, d_up)
    acc_d[...] += contract_rows(c, hidden)

    @pl.when(step == pl.num_programs(0) - 1)
    def _():
        part_ref[0] = acc_g[...].astype(part_ref.dtype)
        part_ref[1] = acc_u[...].astype(part_ref.dtype)
        part_ref[2] = acc_d[...].astype(part_ref.dtype)


def arm_math(tokens, cot, wg, wu, wd):
    rows, width = tokens.shape
    hidden_width = wg.shape[1]
    block = 512
    row_spec = pl.BlockSpec((block, width), lambda i: (i, 0))
    whole = lambda shape: pl.BlockSpec(shape, lambda i: (0, 0))
    flops = 2 * rows * width * hidden_width * 9
    return pl.pallas_call(
        arm_kernel,
        grid=(rows // block,),
        in_specs=[row_spec, row_spec, whole(wg.shape), whole(wu.shape), whole(wd.shape)],
        out_specs=[
            row_spec,
            row_spec,
            pl.BlockSpec((3, width, hidden_width), lambda i: (0, 0, 0)),
        ],
        out_shape=[
            jax.ShapeDtypeStruct((rows, width), jnp.bfloat16),
            jax.ShapeDtypeStruct((rows, width), jnp.bfloat16),
            jax.ShapeDtypeStruct((3, width, hidden_width), jnp.bfloat16),
        ],
        scratch_shapes=[
            pltpu.VMEM((width, hidden_width), jnp.float32),
            pltpu.VMEM((width, hidden_width), jnp.float32),
            pltpu.VMEM((width, hidden_width), jnp.float32),
        ],
        compiler_params=pltpu.CompilerParams(
            dimension_semantics=("arbitrary",), vmem_limit_bytes=48 * 1024 * 1024
        ),
        cost_estimate=pl.CostEstimate(
            flops=flops, bytes_accessed=2 * (4 * rows * width + 6 * width * hidden_width), transcendentals=rows * hidden_width
        ),
    )(tokens, cot, wg, wu, wd)


def reduce_over_dp(partials):
    n = lax.axis_size("dp")
    if n != 4:
        return lax.psum_scatter(partials, "dp", scatter_dimension=2, tiled=True)
    me = lax.axis_index("dp")
    width = partials.shape[2] // n
    rows = partials.shape[1]
    half = rows // 2

    def quarter(offset):
        return lax.dynamic_slice_in_dim(partials, lax.rem(me + offset, n) * width, width, axis=2)

    right = [(i, (i + 1) % n) for i in range(n)]
    left = [(i, (i - 1) % n) for i in range(n)]
    across = quarter(2)
    from_left = lax.ppermute(jnp.concatenate([quarter(1), across[:, :half]], axis=1), "dp", right)
    from_right = lax.ppermute(jnp.concatenate([quarter(n - 1), across[:, half:]], axis=1), "dp", left)
    far_first = lax.ppermute(from_left[:, rows:], "dp", right)
    far_second = lax.ppermute(from_right[:, rows:], "dp", left)
    total = (
        quarter(0).astype(jnp.float32)
        + from_left[:, :rows].astype(jnp.float32)
        + from_right[:, :rows].astype(jnp.float32)
        + jnp.concatenate([far_first, far_second], axis=1).astype(jnp.float32)
    )
    return total.astype(jnp.bfloat16)


def on_device(tokens, codes, cotangent, w_gate, w_up, w_down):
    token_count, feature_width = tokens.shape
    local_arms = w_gate.shape[0]
    arm_count = local_arms * lax.axis_size("expert")
    capacity = 4 * token_count // arm_count
    flat_codes = codes.reshape(-1)
    arm_ids = jnp.arange(arm_count, dtype=jnp.int32)
    onehot = (flat_codes[:, None] == arm_ids[None, :]).astype(jnp.int32)
    earlier = jnp.cumsum(onehot, axis=0) - onehot
    slot = jnp.sum(earlier * onehot, axis=1)
    tok_dest = flat_codes * (2 * capacity) + slot
    cot_dest = tok_dest + capacity
    cot_f = cotangent.astype(jnp.float32)
    sources = jnp.concatenate(
        [tokens, tokens, (cot_f * fact_share).astype(jnp.bfloat16), (cot_f * counter_share).astype(jnp.bfloat16)]
    )
    dest = jnp.concatenate([tok_dest[0::2], tok_dest[1::2], cot_dest[0::2], cot_dest[1::2]])
    place = (
        lax.broadcasted_iota(jnp.int32, (arm_count * 2 * capacity, dest.shape[0]), 0) == dest[None, :]
    ).astype(jnp.bfloat16)
    send = (
        jnp.dot(place, sources, preferred_element_type=jnp.float32)
        .astype(jnp.bfloat16)
        .reshape(arm_count, 2 * capacity, feature_width)
    )
    got = lax.all_to_all(send, "expert", 0, 0, tiled=True)
    arm_tokens = got[:, :capacity].reshape(1, -1, feature_width)
    arm_cot = got[:, capacity:].reshape(1, -1, feature_width)

    out_rows, input_rows, partials = arm_math(
        arm_tokens[0], arm_cot[0], w_gate[0], w_up[0], w_down[0]
    )
    ret = jnp.concatenate(
        [
            out_rows.reshape(-1, capacity, feature_width),
            input_rows.reshape(-1, capacity, feature_width),
        ],
        axis=1,
    )
    back = lax.all_to_all(ret, "expert", 0, 0, tiled=True).reshape(-1, feature_width)
    picked = lax.dot_general(
        place, back, (((0,), (0,)), ((), ())), preferred_element_type=jnp.float32
    ).reshape(4, token_count, feature_width)
    head_output = (fact_share * picked[0] + counter_share * picked[1]).astype(jnp.bfloat16)
    grad_tokens = (picked[2] + picked[3]).astype(jnp.bfloat16)

    summed = reduce_over_dp(partials)
    grad_gate = summed[0:1]
    grad_up = summed[1:2]
    grad_down = summed[2].T[None]
    return (head_output, grad_tokens, grad_gate, grad_up, grad_down)


def solution(mesh):
    return jax.shard_map(
        on_device,
        mesh=mesh,
        in_specs=(
            P(("dp", "expert"), None),
            P(("dp", "expert"), None),
            P(("dp", "expert"), None),
            P("expert", None, None),
            P("expert", None, None),
            P("expert", None, None),
        ),
        out_specs=(
            P(("dp", "expert"), None),
            P(("dp", "expert"), None),
            P("expert", None, "dp"),
            P("expert", None, "dp"),
            P("expert", "dp", None),
        ),
        check_vma=False,
    )
```

```python
import functools

import jax
import jax.numpy as jnp
from jax import lax
from jax.experimental import pallas as pl
from jax.experimental.pallas import tpu as pltpu
from jax.sharding import PartitionSpec as P

fact_share = 0.7
counter_share = 0.3
MESH_ID = pl.DeviceIdType.MESH


def silu_parts(gate_pre):
    sigmoid_gate = jax.nn.sigmoid(gate_pre)
    return (gate_pre * sigmoid_gate, sigmoid_gate * (1.0 + gate_pre * (1.0 - sigmoid_gate)))


def exchange_kernel(n, send_hbm, recv_hbm, send_sem, recv_sem, local_sem):
    me = lax.axis_index("expert")
    row = lax.axis_index("dp")

    def copy_to(i):
        j = lax.rem(me + i, n)
        return pltpu.make_async_remote_copy(
            src_ref=send_hbm.at[j],
            dst_ref=recv_hbm.at[me],
            send_sem=send_sem.at[j],
            recv_sem=recv_sem.at[me],
            device_id=(row, j),
            device_id_type=MESH_ID,
        )

    def start(i, carry):
        copy_to(i).start()
        return carry

    lax.fori_loop(1, n, start, 0)
    local = pltpu.make_async_copy(send_hbm.at[me], recv_hbm.at[me], local_sem)
    local.start()
    local.wait()

    def finish(i, carry):
        j = lax.rem(me + i, n)
        copy_to(i).wait_send()
        pltpu.make_async_remote_copy(
            src_ref=send_hbm.at[j],
            dst_ref=recv_hbm.at[j],
            send_sem=send_sem.at[j],
            recv_sem=recv_sem.at[j],
            device_id=(row, j),
            device_id_type=MESH_ID,
        ).wait_recv()
        return carry

    lax.fori_loop(1, n, finish, 0)


def exchange(send):
    n = send.shape[0]
    nbytes = send.size * send.dtype.itemsize
    return pl.pallas_call(
        functools.partial(exchange_kernel, n),
        out_shape=jax.ShapeDtypeStruct(send.shape, send.dtype),
        in_specs=[pl.BlockSpec(memory_space=pl.ANY)],
        out_specs=pl.BlockSpec(memory_space=pl.ANY),
        scratch_shapes=[
            pltpu.SemaphoreType.DMA((n,)),
            pltpu.SemaphoreType.DMA((n,)),
            pltpu.SemaphoreType.DMA,
        ],
        compiler_params=pltpu.CompilerParams(has_side_effects=True),
        cost_estimate=pl.CostEstimate(flops=0, bytes_accessed=2 * nbytes, transcendentals=0),
    )(send)


def contract_rows(a, b):
    return lax.dot_general(a, b, (((0,), (0,)), ((), ())), preferred_element_type=jnp.float32)


def contract_cols(a, b):
    return lax.dot_general(a, b, (((1,), (1,)), ((), ())), preferred_element_type=jnp.float32)


def arm_kernel(tok_ref, cot_ref, wg_ref, wu_ref, wd_ref, out_ref, inp_ref, part_ref, acc_out, acc_inp):
    step = pl.program_id(0)

    @pl.when(step == 0)
    def _():
        acc_out[...] = jnp.zeros_like(acc_out)
        acc_inp[...] = jnp.zeros_like(acc_inp)

    x = tok_ref[...]
    c = cot_ref[...]
    wg = wg_ref[...]
    wu = wu_ref[...]
    wd = wd_ref[...]
    gate_pre = jnp.dot(x, wg, preferred_element_type=jnp.float32)
    up_pre = jnp.dot(x, wu, preferred_element_type=jnp.float32)
    activated, silu_slope = silu_parts(gate_pre)
    hidden = (activated * up_pre).astype(jnp.bfloat16)
    acc_out[...] += jnp.dot(hidden, wd, preferred_element_type=jnp.float32)
    d_hidden = contract_cols(c, wd)
    d_up = (d_hidden * activated).astype(jnp.bfloat16)
    d_gate = (d_hidden * up_pre * silu_slope).astype(jnp.bfloat16)
    acc_inp[...] += contract_cols(d_gate, wg) + contract_cols(d_up, wu)
    part_ref[0] = contract_rows(x, d_gate).astype(part_ref.dtype)
    part_ref[1] = contract_rows(x, d_up).astype(part_ref.dtype)
    part_ref[2] = contract_rows(c, hidden).astype(part_ref.dtype)

    @pl.when(step == pl.num_programs(0) - 1)
    def _():
        out_ref[...] = acc_out[...].astype(out_ref.dtype)
        inp_ref[...] = acc_inp[...].astype(inp_ref.dtype)


def arm_math(tokens, cot, wg, wu, wd):
    rows, width = tokens.shape
    hidden_width = wg.shape[1]
    chunk = 256
    rows_spec = pl.BlockSpec((rows, width), lambda j: (0, 0))
    flops = 2 * rows * width * hidden_width * 9
    return pl.pallas_call(
        arm_kernel,
        grid=(hidden_width // chunk,),
        in_specs=[
            rows_spec,
            rows_spec,
            pl.BlockSpec((width, chunk), lambda j: (0, j)),
            pl.BlockSpec((width, chunk), lambda j: (0, j)),
            pl.BlockSpec((chunk, width), lambda j: (j, 0)),
        ],
        out_specs=[rows_spec, rows_spec, pl.BlockSpec((3, width, chunk), lambda j: (0, 0, j))],
        out_shape=[
            jax.ShapeDtypeStruct((rows, width), jnp.bfloat16),
            jax.ShapeDtypeStruct((rows, width), jnp.bfloat16),
            jax.ShapeDtypeStruct((3, width, hidden_width), jnp.bfloat16),
        ],
        scratch_shapes=[
            pltpu.VMEM((rows, width), jnp.float32),
            pltpu.VMEM((rows, width), jnp.float32),
        ],
        compiler_params=pltpu.CompilerParams(
            dimension_semantics=("arbitrary",), vmem_limit_bytes=48 * 1024 * 1024
        ),
        cost_estimate=pl.CostEstimate(
            flops=flops, bytes_accessed=2 * (4 * rows * width + 6 * width * hidden_width), transcendentals=rows * hidden_width
        ),
    )(tokens, cot, wg, wu, wd)

def on_device(tokens, codes, cotangent, w_gate, w_up, w_down):
    token_count, feature_width = tokens.shape
    local_arms = w_gate.shape[0]
    arm_count = local_arms * lax.axis_size("expert")
    capacity = 4 * token_count // arm_count
    flat_codes = codes.reshape(-1)
    arm_ids = jnp.arange(arm_count, dtype=jnp.int32)
    onehot = (flat_codes[:, None] == arm_ids[None, :]).astype(jnp.int32)
    earlier = jnp.cumsum(onehot, axis=0) - onehot
    slot = jnp.sum(earlier * onehot, axis=1)
    tok_dest = flat_codes * (2 * capacity) + slot
    cot_dest = tok_dest + capacity
    cot_f = cotangent.astype(jnp.float32)
    sources = jnp.concatenate(
        [tokens, tokens, (cot_f * fact_share).astype(jnp.bfloat16), (cot_f * counter_share).astype(jnp.bfloat16)]
    )
    dest = jnp.concatenate([tok_dest[0::2], tok_dest[1::2], cot_dest[0::2], cot_dest[1::2]])
    place = (
        lax.broadcasted_iota(jnp.int32, (arm_count * 2 * capacity, dest.shape[0]), 0) == dest[None, :]
    ).astype(jnp.bfloat16)
    send = (
        jnp.dot(place, sources, preferred_element_type=jnp.float32)
        .astype(jnp.bfloat16)
        .reshape(arm_count, 2 * capacity, feature_width)
    )
    got = lax.all_to_all(send, "expert", 0, 0, tiled=True)
    arm_tokens = got[:, :capacity].reshape(1, -1, feature_width)
    arm_cot = got[:, capacity:].reshape(1, -1, feature_width)

    out_rows, input_rows, partials = arm_math(
        arm_tokens[0], arm_cot[0], w_gate[0], w_up[0], w_down[0]
    )
    ret = jnp.concatenate(
        [
            out_rows.reshape(-1, capacity, feature_width),
            input_rows.reshape(-1, capacity, feature_width),
        ],
        axis=1,
    )
    back = lax.all_to_all(ret, "expert", 0, 0, tiled=True).reshape(-1, feature_width)
    picked = lax.dot_general(
        place, back, (((0,), (0,)), ((), ())), preferred_element_type=jnp.float32
    ).reshape(4, token_count, feature_width)
    head_output = (fact_share * picked[0] + counter_share * picked[1]).astype(jnp.bfloat16)
    grad_tokens = (picked[2] + picked[3]).astype(jnp.bfloat16)

    summed = lax.psum_scatter(partials, "dp", scatter_dimension=2, tiled=True)
    grad_gate = summed[0:1]
    grad_up = summed[1:2]
    grad_down = summed[2].T[None]
    return (head_output, grad_tokens, grad_gate, grad_up, grad_down)


def solution(mesh):
    return jax.shard_map(
        on_device,
        mesh=mesh,
        in_specs=(
            P(("dp", "expert"), None),
            P(("dp", "expert"), None),
            P(("dp", "expert"), None),
            P("expert", None, None),
            P("expert", None, None),
            P("expert", None, None),
        ),
        out_specs=(
            P(("dp", "expert"), None),
            P(("dp", "expert"), None),
            P("expert", None, "dp"),
            P("expert", None, "dp"),
            P("expert", "dp", None),
        ),
        check_vma=False,
    )
```

```python
import functools

import jax
import jax.numpy as jnp
from jax import lax
from jax.experimental import pallas as pl
from jax.experimental.pallas import tpu as pltpu
from jax.sharding import PartitionSpec as P

fact_share = 0.7
counter_share = 0.3
MESH_ID = pl.DeviceIdType.MESH


def silu_parts(gate_pre):
    sigmoid_gate = jax.nn.sigmoid(gate_pre)
    return (gate_pre * sigmoid_gate, sigmoid_gate * (1.0 + gate_pre * (1.0 - sigmoid_gate)))


def exchange_kernel(n, send_hbm, recv_hbm, send_sem, recv_sem, local_sem):
    me = lax.axis_index("expert")
    row = lax.axis_index("dp")

    def copy_to(i):
        j = lax.rem(me + i, n)
        return pltpu.make_async_remote_copy(
            src_ref=send_hbm.at[j],
            dst_ref=recv_hbm.at[me],
            send_sem=send_sem.at[j],
            recv_sem=recv_sem.at[me],
            device_id=(row, j),
            device_id_type=MESH_ID,
        )

    def start(i, carry):
        copy_to(i).start()
        return carry

    lax.fori_loop(1, n, start, 0)
    local = pltpu.make_async_copy(send_hbm.at[me], recv_hbm.at[me], local_sem)
    local.start()
    local.wait()

    def finish(i, carry):
        j = lax.rem(me + i, n)
        copy_to(i).wait_send()
        pltpu.make_async_remote_copy(
            src_ref=send_hbm.at[j],
            dst_ref=recv_hbm.at[j],
            send_sem=send_sem.at[j],
            recv_sem=recv_sem.at[j],
            device_id=(row, j),
            device_id_type=MESH_ID,
        ).wait_recv()
        return carry

    lax.fori_loop(1, n, finish, 0)


def exchange(send):
    n = send.shape[0]
    nbytes = send.size * send.dtype.itemsize
    return pl.pallas_call(
        functools.partial(exchange_kernel, n),
        out_shape=jax.ShapeDtypeStruct(send.shape, send.dtype),
        in_specs=[pl.BlockSpec(memory_space=pl.ANY)],
        out_specs=pl.BlockSpec(memory_space=pl.ANY),
        scratch_shapes=[
            pltpu.SemaphoreType.DMA((n,)),
            pltpu.SemaphoreType.DMA((n,)),
            pltpu.SemaphoreType.DMA,
        ],
        compiler_params=pltpu.CompilerParams(has_side_effects=True),
        cost_estimate=pl.CostEstimate(flops=0, bytes_accessed=2 * nbytes, transcendentals=0),
    )(send)


def contract_rows(a, b):
    return lax.dot_general(a, b, (((0,), (0,)), ((), ())), preferred_element_type=jnp.float32)


def contract_cols(a, b):
    return lax.dot_general(a, b, (((1,), (1,)), ((), ())), preferred_element_type=jnp.float32)


def arm_kernel(tok_ref, cot_ref, wg_ref, wu_ref, wd_ref, out_ref, inp_ref, part_ref, acc_g, acc_u, acc_d):
    step = pl.program_id(0)
    hidden_width = wg_ref.shape[1]

    @pl.when(step == 0)
    def _():
        acc_g[...] = jnp.zeros_like(acc_g)
        acc_u[...] = jnp.zeros_like(acc_u)
        acc_d[...] = jnp.zeros_like(acc_d)

    x = tok_ref[...]
    c = cot_ref[...]
    wg = wg_ref[...]
    wu = wu_ref[...]
    wd = wd_ref[...]
    gate_pre = jnp.dot(x, wg, preferred_element_type=jnp.float32)
    up_pre = jnp.dot(x, wu, preferred_element_type=jnp.float32)
    activated, silu_slope = silu_parts(gate_pre)
    hidden = (activated * up_pre).astype(jnp.bfloat16)
    out_ref[...] = jnp.dot(hidden, wd, preferred_element_type=jnp.float32).astype(out_ref.dtype)
    d_hidden = contract_cols(c, wd)
    d_up = (d_hidden * activated).astype(jnp.bfloat16)
    d_gate = (d_hidden * up_pre * silu_slope).astype(jnp.bfloat16)
    inp_ref[...] = (contract_cols(d_gate, wg) + contract_cols(d_up, wu)).astype(inp_ref.dtype)
    acc_g[...] += contract_rows(x, d_gate)
    acc_u[...] += contract_rows(x, d_up)
    acc_d[...] += contract_rows(c, hidden)

    @pl.when(step == pl.num_programs(0) - 1)
    def _():
        part_ref[0] = acc_g[...].astype(part_ref.dtype)
        part_ref[1] = acc_u[...].astype(part_ref.dtype)
        part_ref[2] = acc_d[...].astype(part_ref.dtype)


def arm_math(tokens, cot, wg, wu, wd):
    rows, width = tokens.shape
    hidden_width = wg.shape[1]
    block = 512
    row_spec = pl.BlockSpec((block, width), lambda i: (i, 0))
    whole = lambda shape: pl.BlockSpec(shape, lambda i: (0, 0))
    flops = 2 * rows * width * hidden_width * 9
    return pl.pallas_call(
        arm_kernel,
        grid=(rows // block,),
        in_specs=[row_spec, row_spec, whole(wg.shape), whole(wu.shape), whole(wd.shape)],
        out_specs=[
            row_spec,
            row_spec,
            pl.BlockSpec((3, width, hidden_width), lambda i: (0, 0, 0)),
        ],
        out_shape=[
            jax.ShapeDtypeStruct((rows, width), jnp.bfloat16),
            jax.ShapeDtypeStruct((rows, width), jnp.bfloat16),
            jax.ShapeDtypeStruct((3, width, hidden_width), jnp.bfloat16),
        ],
        scratch_shapes=[
            pltpu.VMEM((width, hidden_width), jnp.float32),
            pltpu.VMEM((width, hidden_width), jnp.float32),
            pltpu.VMEM((width, hidden_width), jnp.float32),
        ],
        compiler_params=pltpu.CompilerParams(
            dimension_semantics=("arbitrary",), vmem_limit_bytes=48 * 1024 * 1024
        ),
        cost_estimate=pl.CostEstimate(
            flops=flops, bytes_accessed=2 * (4 * rows * width + 6 * width * hidden_width), transcendentals=rows * hidden_width
        ),
    )(tokens, cot, wg, wu, wd)


def split_kernel(summed_ref, gate_ref, up_ref, down_ref):
    gate_ref[...] = summed_ref[0]
    up_ref[...] = summed_ref[1]
    down_ref[...] = summed_ref[2].astype(jnp.float32).T.astype(down_ref.dtype)


def split_grads(summed):
    _, width, part = summed.shape
    vmem = pl.BlockSpec(memory_space=pltpu.VMEM)
    return pl.pallas_call(
        split_kernel,
        in_specs=[vmem],
        out_specs=[vmem, vmem, vmem],
        out_shape=[
            jax.ShapeDtypeStruct((width, part), summed.dtype),
            jax.ShapeDtypeStruct((width, part), summed.dtype),
            jax.ShapeDtypeStruct((part, width), summed.dtype),
        ],
    )(summed)


def on_device(tokens, codes, cotangent, w_gate, w_up, w_down):
    token_count, feature_width = tokens.shape
    local_arms = w_gate.shape[0]
    arm_count = local_arms * lax.axis_size("expert")
    capacity = 4 * token_count // arm_count
    flat_codes = codes.reshape(-1)
    arm_ids = jnp.arange(arm_count, dtype=jnp.int32)
    onehot = (flat_codes[:, None] == arm_ids[None, :]).astype(jnp.int32)
    earlier = jnp.cumsum(onehot, axis=0) - onehot
    slot = jnp.sum(earlier * onehot, axis=1)
    tok_dest = flat_codes * (2 * capacity) + slot
    cot_dest = tok_dest + capacity
    cot_f = cotangent.astype(jnp.float32)
    sources = jnp.concatenate(
        [tokens, tokens, (cot_f * fact_share).astype(jnp.bfloat16), (cot_f * counter_share).astype(jnp.bfloat16)]
    )
    dest = jnp.concatenate([tok_dest[0::2], tok_dest[1::2], cot_dest[0::2], cot_dest[1::2]])
    place = (
        lax.broadcasted_iota(jnp.int32, (arm_count * 2 * capacity, dest.shape[0]), 0) == dest[None, :]
    ).astype(jnp.bfloat16)
    send = (
        jnp.dot(place, sources, preferred_element_type=jnp.float32)
        .astype(jnp.bfloat16)
        .reshape(arm_count, 2 * capacity, feature_width)
    )
    got = lax.all_to_all(send, "expert", 0, 0, tiled=True)
    arm_tokens = got[:, :capacity].reshape(1, -1, feature_width)
    arm_cot = got[:, capacity:].reshape(1, -1, feature_width)

    out_rows, input_rows, partials = arm_math(
        arm_tokens[0], arm_cot[0], w_gate[0], w_up[0], w_down[0]
    )
    ret = jnp.concatenate(
        [
            out_rows.reshape(-1, capacity, feature_width),
            input_rows.reshape(-1, capacity, feature_width),
        ],
        axis=1,
    )
    back = lax.all_to_all(ret, "expert", 0, 0, tiled=True).reshape(-1, feature_width)
    picked = lax.dot_general(
        place, back, (((0,), (0,)), ((), ())), preferred_element_type=jnp.float32
    ).reshape(4, token_count, feature_width)
    head_output = (fact_share * picked[0] + counter_share * picked[1]).astype(jnp.bfloat16)
    grad_tokens = (picked[2] + picked[3]).astype(jnp.bfloat16)

    summed = lax.psum_scatter(partials, "dp", scatter_dimension=2, tiled=True)
    grad_gate, grad_up, grad_down = (g[None] for g in split_grads(summed))
    return (head_output, grad_tokens, grad_gate, grad_up, grad_down)


def solution(mesh):
    return jax.shard_map(
        on_device,
        mesh=mesh,
        in_specs=(
            P(("dp", "expert"), None),
            P(("dp", "expert"), None),
            P(("dp", "expert"), None),
            P("expert", None, None),
            P("expert", None, None),
            P("expert", None, None),
        ),
        out_specs=(
            P(("dp", "expert"), None),
            P(("dp", "expert"), None),
            P("expert", None, "dp"),
            P("expert", None, "dp"),
            P("expert", "dp", None),
        ),
        check_vma=False,
    )
```

```python
import functools

import jax
import jax.numpy as jnp
from jax import lax
from jax.experimental import pallas as pl
from jax.experimental.pallas import tpu as pltpu
from jax.sharding import PartitionSpec as P

fact_share = 0.7
counter_share = 0.3
MESH_ID = pl.DeviceIdType.MESH


def silu_parts(gate_pre):
    sigmoid_gate = jax.nn.sigmoid(gate_pre)
    return (gate_pre * sigmoid_gate, sigmoid_gate * (1.0 + gate_pre * (1.0 - sigmoid_gate)))


def exchange_kernel(n, send_hbm, recv_hbm, send_sem, recv_sem, local_sem):
    me = lax.axis_index("expert")
    row = lax.axis_index("dp")

    def copy_to(i):
        j = lax.rem(me + i, n)
        return pltpu.make_async_remote_copy(
            src_ref=send_hbm.at[j],
            dst_ref=recv_hbm.at[me],
            send_sem=send_sem.at[j],
            recv_sem=recv_sem.at[me],
            device_id=(row, j),
            device_id_type=MESH_ID,
        )

    def start(i, carry):
        copy_to(i).start()
        return carry

    lax.fori_loop(1, n, start, 0)
    local = pltpu.make_async_copy(send_hbm.at[me], recv_hbm.at[me], local_sem)
    local.start()
    local.wait()

    def finish(i, carry):
        j = lax.rem(me + i, n)
        copy_to(i).wait_send()
        pltpu.make_async_remote_copy(
            src_ref=send_hbm.at[j],
            dst_ref=recv_hbm.at[j],
            send_sem=send_sem.at[j],
            recv_sem=recv_sem.at[j],
            device_id=(row, j),
            device_id_type=MESH_ID,
        ).wait_recv()
        return carry

    lax.fori_loop(1, n, finish, 0)


def exchange(send):
    n = send.shape[0]
    nbytes = send.size * send.dtype.itemsize
    return pl.pallas_call(
        functools.partial(exchange_kernel, n),
        out_shape=jax.ShapeDtypeStruct(send.shape, send.dtype),
        in_specs=[pl.BlockSpec(memory_space=pl.ANY)],
        out_specs=pl.BlockSpec(memory_space=pl.ANY),
        scratch_shapes=[
            pltpu.SemaphoreType.DMA((n,)),
            pltpu.SemaphoreType.DMA((n,)),
            pltpu.SemaphoreType.DMA,
        ],
        compiler_params=pltpu.CompilerParams(has_side_effects=True),
        cost_estimate=pl.CostEstimate(flops=0, bytes_accessed=2 * nbytes, transcendentals=0),
    )(send)


def contract_rows(a, b):
    return lax.dot_general(a, b, (((0,), (0,)), ((), ())), preferred_element_type=jnp.float32)


def contract_cols(a, b):
    return lax.dot_general(a, b, (((1,), (1,)), ((), ())), preferred_element_type=jnp.float32)


def arm_kernel(tok_ref, cot_ref, wg_ref, wu_ref, wd_ref, out_ref, inp_ref, part_ref, acc_g, acc_u, acc_d):
    step = pl.program_id(0)
    hidden_width = wg_ref.shape[1]

    @pl.when(step == 0)
    def _():
        acc_g[...] = jnp.zeros_like(acc_g)
        acc_u[...] = jnp.zeros_like(acc_u)
        acc_d[...] = jnp.zeros_like(acc_d)

    x = tok_ref[...]
    c = cot_ref[...]
    wg = wg_ref[...]
    wu = wu_ref[...]
    wd = wd_ref[...]
    gate_pre = jnp.dot(x, wg, preferred_element_type=jnp.float32)
    up_pre = jnp.dot(x, wu, preferred_element_type=jnp.float32)
    activated, silu_slope = silu_parts(gate_pre)
    hidden = (activated * up_pre).astype(jnp.bfloat16)
    out_ref[...] = jnp.dot(hidden, wd, preferred_element_type=jnp.float32).astype(out_ref.dtype)
    d_hidden = contract_cols(c, wd)
    d_up = (d_hidden * activated).astype(jnp.bfloat16)
    d_gate = (d_hidden * up_pre * silu_slope).astype(jnp.bfloat16)
    inp_ref[...] = (contract_cols(d_gate, wg) + contract_cols(d_up, wu)).astype(inp_ref.dtype)
    acc_g[...] += contract_rows(x, d_gate)
    acc_u[...] += contract_rows(x, d_up)
    acc_d[...] += contract_rows(c, hidden)

    @pl.when(step == pl.num_programs(0) - 1)
    def _():
        part_ref[0] = acc_g[...].astype(part_ref.dtype)
        part_ref[1] = acc_u[...].astype(part_ref.dtype)
        part_ref[2] = acc_d[...].astype(part_ref.dtype)


def arm_math(tokens, cot, wg, wu, wd):
    rows, width = tokens.shape
    hidden_width = wg.shape[1]
    block = 512
    row_spec = pl.BlockSpec((block, width), lambda i: (i, 0))
    whole = lambda shape: pl.BlockSpec(shape, lambda i: (0, 0))
    flops = 2 * rows * width * hidden_width * 9
    return pl.pallas_call(
        arm_kernel,
        grid=(rows // block,),
        in_specs=[row_spec, row_spec, whole(wg.shape), whole(wu.shape), whole(wd.shape)],
        out_specs=[
            row_spec,
            row_spec,
            pl.BlockSpec((3, width, hidden_width), lambda i: (0, 0, 0)),
        ],
        out_shape=[
            jax.ShapeDtypeStruct((rows, width), jnp.bfloat16),
            jax.ShapeDtypeStruct((rows, width), jnp.bfloat16),
            jax.ShapeDtypeStruct((3, width, hidden_width), jnp.bfloat16),
        ],
        scratch_shapes=[
            pltpu.VMEM((width, hidden_width), jnp.float32),
            pltpu.VMEM((width, hidden_width), jnp.float32),
            pltpu.VMEM((width, hidden_width), jnp.float32),
        ],
        compiler_params=pltpu.CompilerParams(
            dimension_semantics=("arbitrary",), vmem_limit_bytes=48 * 1024 * 1024
        ),
        cost_estimate=pl.CostEstimate(
            flops=flops, bytes_accessed=2 * (4 * rows * width + 6 * width * hidden_width), transcendentals=rows * hidden_width
        ),
    )(tokens, cot, wg, wu, wd)


def split_kernel(summed_ref, gate_ref, up_ref, down_ref):
    gate_ref[...] = summed_ref[0]
    up_ref[...] = summed_ref[1]
    down_ref[...] = summed_ref[2].astype(jnp.float32).T.astype(down_ref.dtype)


def split_grads(summed):
    _, width, part = summed.shape
    vmem = pl.BlockSpec(memory_space=pltpu.VMEM)
    return pl.pallas_call(
        split_kernel,
        in_specs=[vmem],
        out_specs=[vmem, vmem, vmem],
        out_shape=[
            jax.ShapeDtypeStruct((width, part), summed.dtype),
            jax.ShapeDtypeStruct((width, part), summed.dtype),
            jax.ShapeDtypeStruct((part, width), summed.dtype),
        ],
    )(summed)


def on_device(tokens, codes, cotangent, w_gate, w_up, w_down):
    token_count, feature_width = tokens.shape
    local_arms = w_gate.shape[0]
    arm_count = local_arms * lax.axis_size("expert")
    capacity = 4 * token_count // arm_count
    flat_codes = codes.T.reshape(-1)
    arm_ids = jnp.arange(arm_count, dtype=jnp.int32)
    onehot = (flat_codes[:, None] == arm_ids[None, :]).astype(jnp.int32)
    earlier = jnp.cumsum(onehot, axis=0) - onehot
    slot = jnp.sum(earlier * onehot, axis=1)
    tok_dest = flat_codes * (2 * capacity) + slot
    cot_dest = tok_dest + capacity
    cot_f = cotangent.astype(jnp.float32)
    sources = jnp.concatenate(
        [tokens, tokens, (cot_f * fact_share).astype(jnp.bfloat16), (cot_f * counter_share).astype(jnp.bfloat16)]
    )
    dest = jnp.concatenate([tok_dest, cot_dest])
    place = (
        lax.broadcasted_iota(jnp.int32, (arm_count * 2 * capacity, dest.shape[0]), 0) == dest[None, :]
    ).astype(jnp.bfloat16)
    send = (
        jnp.dot(place, sources, preferred_element_type=jnp.float32)
        .astype(jnp.bfloat16)
        .reshape(arm_count, 2 * capacity, feature_width)
    )
    got = lax.all_to_all(send, "expert", 0, 0, tiled=True)
    arm_tokens = got[:, :capacity].reshape(1, -1, feature_width)
    arm_cot = got[:, capacity:].reshape(1, -1, feature_width)

    out_rows, input_rows, partials = arm_math(
        arm_tokens[0], arm_cot[0], w_gate[0], w_up[0], w_down[0]
    )
    ret = jnp.concatenate(
        [
            out_rows.reshape(-1, capacity, feature_width),
            input_rows.reshape(-1, capacity, feature_width),
        ],
        axis=1,
    )
    back = lax.all_to_all(ret, "expert", 0, 0, tiled=True).reshape(-1, feature_width)
    picked = lax.dot_general(
        place, back, (((0,), (0,)), ((), ())), preferred_element_type=jnp.float32
    ).reshape(4, token_count, feature_width)
    head_output = (fact_share * picked[0] + counter_share * picked[1]).astype(jnp.bfloat16)
    grad_tokens = (picked[2] + picked[3]).astype(jnp.bfloat16)

    summed = lax.psum_scatter(partials, "dp", scatter_dimension=2, tiled=True)
    grad_gate, grad_up, grad_down = (g[None] for g in split_grads(summed))
    return (head_output, grad_tokens, grad_gate, grad_up, grad_down)


def solution(mesh):
    return jax.shard_map(
        on_device,
        mesh=mesh,
        in_specs=(
            P(("dp", "expert"), None),
            P(("dp", "expert"), None),
            P(("dp", "expert"), None),
            P("expert", None, None),
            P("expert", None, None),
            P("expert", None, None),
        ),
        out_specs=(
            P(("dp", "expert"), None),
            P(("dp", "expert"), None),
            P("expert", None, "dp"),
            P("expert", None, "dp"),
            P("expert", "dp", None),
        ),
        check_vma=False,
    )
```

```python
import functools

import jax
import jax.numpy as jnp
from jax import lax
from jax.experimental import pallas as pl
from jax.experimental.pallas import tpu as pltpu
from jax.sharding import PartitionSpec as P

fact_share = 0.7
counter_share = 0.3
MESH_ID = pl.DeviceIdType.MESH


def silu_parts(gate_pre):
    sigmoid_gate = jax.nn.sigmoid(gate_pre)
    return (gate_pre * sigmoid_gate, sigmoid_gate * (1.0 + gate_pre * (1.0 - sigmoid_gate)))


def exchange_kernel(n, send_hbm, recv_hbm, send_sem, recv_sem, local_sem):
    me = lax.axis_index("expert")
    row = lax.axis_index("dp")

    def copy_to(i):
        j = lax.rem(me + i, n)
        return pltpu.make_async_remote_copy(
            src_ref=send_hbm.at[j],
            dst_ref=recv_hbm.at[me],
            send_sem=send_sem.at[j],
            recv_sem=recv_sem.at[me],
            device_id=(row, j),
            device_id_type=MESH_ID,
        )

    def start(i, carry):
        copy_to(i).start()
        return carry

    lax.fori_loop(1, n, start, 0)
    local = pltpu.make_async_copy(send_hbm.at[me], recv_hbm.at[me], local_sem)
    local.start()
    local.wait()

    def finish(i, carry):
        j = lax.rem(me + i, n)
        copy_to(i).wait_send()
        pltpu.make_async_remote_copy(
            src_ref=send_hbm.at[j],
            dst_ref=recv_hbm.at[j],
            send_sem=send_sem.at[j],
            recv_sem=recv_sem.at[j],
            device_id=(row, j),
            device_id_type=MESH_ID,
        ).wait_recv()
        return carry

    lax.fori_loop(1, n, finish, 0)


def exchange(send):
    n = send.shape[0]
    nbytes = send.size * send.dtype.itemsize
    return pl.pallas_call(
        functools.partial(exchange_kernel, n),
        out_shape=jax.ShapeDtypeStruct(send.shape, send.dtype),
        in_specs=[pl.BlockSpec(memory_space=pl.ANY)],
        out_specs=pl.BlockSpec(memory_space=pl.ANY),
        scratch_shapes=[
            pltpu.SemaphoreType.DMA((n,)),
            pltpu.SemaphoreType.DMA((n,)),
            pltpu.SemaphoreType.DMA,
        ],
        compiler_params=pltpu.CompilerParams(has_side_effects=True),
        cost_estimate=pl.CostEstimate(flops=0, bytes_accessed=2 * nbytes, transcendentals=0),
    )(send)


def contract_rows(a, b):
    return lax.dot_general(a, b, (((0,), (0,)), ((), ())), preferred_element_type=jnp.float32)


def contract_cols(a, b):
    return lax.dot_general(a, b, (((1,), (1,)), ((), ())), preferred_element_type=jnp.float32)


def arm_kernel(tok_ref, cot_ref, wg_ref, wu_ref, wd_ref, out_ref, inp_ref, part_ref, acc_g, acc_u, acc_d):
    step = pl.program_id(0)
    hidden_width = wg_ref.shape[1]

    @pl.when(step == 0)
    def _():
        acc_g[...] = jnp.zeros_like(acc_g)
        acc_u[...] = jnp.zeros_like(acc_u)
        acc_d[...] = jnp.zeros_like(acc_d)

    x = tok_ref[...]
    c = cot_ref[...]
    wg = wg_ref[...]
    wu = wu_ref[...]
    wd = wd_ref[...]
    gate_pre = jnp.dot(x, wg, preferred_element_type=jnp.float32)
    up_pre = jnp.dot(x, wu, preferred_element_type=jnp.float32)
    activated, silu_slope = silu_parts(gate_pre)
    hidden = (activated * up_pre).astype(jnp.bfloat16)
    out_ref[...] = jnp.dot(hidden, wd, preferred_element_type=jnp.float32).astype(out_ref.dtype)
    d_hidden = contract_cols(c, wd)
    d_up = (d_hidden * activated).astype(jnp.bfloat16)
    d_gate = (d_hidden * up_pre * silu_slope).astype(jnp.bfloat16)
    inp_ref[...] = (contract_cols(d_gate, wg) + contract_cols(d_up, wu)).astype(inp_ref.dtype)
    acc_g[...] += contract_rows(x, d_gate)
    acc_u[...] += contract_rows(x, d_up)
    acc_d[...] += contract_rows(c, hidden)

    @pl.when(step == pl.num_programs(0) - 1)
    def _():
        part_ref[0] = acc_g[...].astype(part_ref.dtype)
        part_ref[1] = acc_u[...].astype(part_ref.dtype)
        part_ref[2] = acc_d[...].astype(part_ref.dtype)


def arm_math(tokens, cot, wg, wu, wd):
    rows, width = tokens.shape
    hidden_width = wg.shape[1]
    block = 512
    row_spec = pl.BlockSpec((block, width), lambda i: (i, 0))
    whole = lambda shape: pl.BlockSpec(shape, lambda i: (0, 0))
    flops = 2 * rows * width * hidden_width * 9
    return pl.pallas_call(
        arm_kernel,
        grid=(rows // block,),
        in_specs=[row_spec, row_spec, whole(wg.shape), whole(wu.shape), whole(wd.shape)],
        out_specs=[
            row_spec,
            row_spec,
            pl.BlockSpec((3, width, hidden_width), lambda i: (0, 0, 0)),
        ],
        out_shape=[
            jax.ShapeDtypeStruct((rows, width), jnp.bfloat16),
            jax.ShapeDtypeStruct((rows, width), jnp.bfloat16),
            jax.ShapeDtypeStruct((3, width, hidden_width), jnp.bfloat16),
        ],
        scratch_shapes=[
            pltpu.VMEM((width, hidden_width), jnp.float32),
            pltpu.VMEM((width, hidden_width), jnp.float32),
            pltpu.VMEM((width, hidden_width), jnp.float32),
        ],
        compiler_params=pltpu.CompilerParams(
            dimension_semantics=("arbitrary",), vmem_limit_bytes=48 * 1024 * 1024
        ),
        cost_estimate=pl.CostEstimate(
            flops=flops, bytes_accessed=2 * (4 * rows * width + 6 * width * hidden_width), transcendentals=rows * hidden_width
        ),
    )(tokens, cot, wg, wu, wd)


def split_kernel(summed_ref, gate_ref, up_ref, down_ref):
    gate_ref[...] = summed_ref[0]
    up_ref[...] = summed_ref[1]
    down_ref[...] = summed_ref[2].astype(jnp.float32).T.astype(down_ref.dtype)


def split_grads(summed):
    _, width, part = summed.shape
    vmem = pl.BlockSpec(memory_space=pltpu.VMEM)
    return pl.pallas_call(
        split_kernel,
        in_specs=[vmem],
        out_specs=[vmem, vmem, vmem],
        out_shape=[
            jax.ShapeDtypeStruct((width, part), summed.dtype),
            jax.ShapeDtypeStruct((width, part), summed.dtype),
            jax.ShapeDtypeStruct((part, width), summed.dtype),
        ],
    )(summed)


def on_device(tokens, codes, cotangent, w_gate, w_up, w_down):
    token_count, feature_width = tokens.shape
    local_arms = w_gate.shape[0]
    arm_count = local_arms * lax.axis_size("expert")
    capacity = 4 * token_count // arm_count
    flat_codes = codes.T.reshape(-1)
    arm_ids = jnp.arange(arm_count, dtype=jnp.int32)
    onehot = (flat_codes[:, None] == arm_ids[None, :]).astype(jnp.bfloat16)
    count = flat_codes.shape[0]
    before = (
        lax.broadcasted_iota(jnp.int32, (count, count), 1)
        < lax.broadcasted_iota(jnp.int32, (count, count), 0)
    ).astype(jnp.bfloat16)
    earlier = jnp.dot(before, onehot, preferred_element_type=jnp.float32)
    slot = jnp.sum(earlier * onehot.astype(jnp.float32), axis=1).astype(jnp.int32)
    tok_dest = flat_codes * (2 * capacity) + slot
    cot_dest = tok_dest + capacity
    cot_f = cotangent.astype(jnp.float32)
    sources = jnp.concatenate(
        [tokens, tokens, (cot_f * fact_share).astype(jnp.bfloat16), (cot_f * counter_share).astype(jnp.bfloat16)]
    )
    dest = jnp.concatenate([tok_dest, cot_dest])
    place = (
        lax.broadcasted_iota(jnp.int32, (arm_count * 2 * capacity, dest.shape[0]), 0) == dest[None, :]
    ).astype(jnp.bfloat16)
    send = (
        jnp.dot(place, sources, preferred_element_type=jnp.float32)
        .astype(jnp.bfloat16)
        .reshape(arm_count, 2 * capacity, feature_width)
    )
    got = lax.all_to_all(send, "expert", 0, 0, tiled=True)
    arm_tokens = got[:, :capacity].reshape(1, -1, feature_width)
    arm_cot = got[:, capacity:].reshape(1, -1, feature_width)

    out_rows, input_rows, partials = arm_math(
        arm_tokens[0], arm_cot[0], w_gate[0], w_up[0], w_down[0]
    )
    ret = jnp.concatenate(
        [
            out_rows.reshape(-1, capacity, feature_width),
            input_rows.reshape(-1, capacity, feature_width),
        ],
        axis=1,
    )
    back = lax.all_to_all(ret, "expert", 0, 0, tiled=True).reshape(-1, feature_width)
    picked = lax.dot_general(
        place, back, (((0,), (0,)), ((), ())), preferred_element_type=jnp.float32
    ).reshape(4, token_count, feature_width)
    head_output = (fact_share * picked[0] + counter_share * picked[1]).astype(jnp.bfloat16)
    grad_tokens = (picked[2] + picked[3]).astype(jnp.bfloat16)

    summed = lax.psum_scatter(partials, "dp", scatter_dimension=2, tiled=True)
    grad_gate, grad_up, grad_down = (g[None] for g in split_grads(summed))
    return (head_output, grad_tokens, grad_gate, grad_up, grad_down)


def solution(mesh):
    return jax.shard_map(
        on_device,
        mesh=mesh,
        in_specs=(
            P(("dp", "expert"), None),
            P(("dp", "expert"), None),
            P(("dp", "expert"), None),
            P("expert", None, None),
            P("expert", None, None),
            P("expert", None, None),
        ),
        out_specs=(
            P(("dp", "expert"), None),
            P(("dp", "expert"), None),
            P("expert", None, "dp"),
            P("expert", None, "dp"),
            P("expert", "dp", None),
        ),
        check_vma=False,
    )
```

```python
import functools

import jax
import jax.numpy as jnp
from jax import lax
from jax.experimental import pallas as pl
from jax.experimental.pallas import tpu as pltpu
from jax.sharding import PartitionSpec as P

fact_share = 0.7
counter_share = 0.3
MESH_ID = pl.DeviceIdType.MESH


def silu_parts(gate_pre):
    sigmoid_gate = jax.nn.sigmoid(gate_pre)
    return (gate_pre * sigmoid_gate, sigmoid_gate * (1.0 + gate_pre * (1.0 - sigmoid_gate)))


def exchange_kernel(n, send_hbm, recv_hbm, send_sem, recv_sem, local_sem):
    me = lax.axis_index("expert")
    row = lax.axis_index("dp")

    def copy_to(i):
        j = lax.rem(me + i, n)
        return pltpu.make_async_remote_copy(
            src_ref=send_hbm.at[j],
            dst_ref=recv_hbm.at[me],
            send_sem=send_sem.at[j],
            recv_sem=recv_sem.at[me],
            device_id=(row, j),
            device_id_type=MESH_ID,
        )

    def start(i, carry):
        copy_to(i).start()
        return carry

    lax.fori_loop(1, n, start, 0)
    local = pltpu.make_async_copy(send_hbm.at[me], recv_hbm.at[me], local_sem)
    local.start()
    local.wait()

    def finish(i, carry):
        j = lax.rem(me + i, n)
        copy_to(i).wait_send()
        pltpu.make_async_remote_copy(
            src_ref=send_hbm.at[j],
            dst_ref=recv_hbm.at[j],
            send_sem=send_sem.at[j],
            recv_sem=recv_sem.at[j],
            device_id=(row, j),
            device_id_type=MESH_ID,
        ).wait_recv()
        return carry

    lax.fori_loop(1, n, finish, 0)


def exchange(send):
    n = send.shape[0]
    nbytes = send.size * send.dtype.itemsize
    return pl.pallas_call(
        functools.partial(exchange_kernel, n),
        out_shape=jax.ShapeDtypeStruct(send.shape, send.dtype),
        in_specs=[pl.BlockSpec(memory_space=pl.ANY)],
        out_specs=pl.BlockSpec(memory_space=pl.ANY),
        scratch_shapes=[
            pltpu.SemaphoreType.DMA((n,)),
            pltpu.SemaphoreType.DMA((n,)),
            pltpu.SemaphoreType.DMA,
        ],
        compiler_params=pltpu.CompilerParams(has_side_effects=True),
        cost_estimate=pl.CostEstimate(flops=0, bytes_accessed=2 * nbytes, transcendentals=0),
    )(send)


def contract_rows(a, b):
    return lax.dot_general(a, b, (((0,), (0,)), ((), ())), preferred_element_type=jnp.float32)


def contract_cols(a, b):
    return lax.dot_general(a, b, (((1,), (1,)), ((), ())), preferred_element_type=jnp.float32)


def arm_kernel(tok_ref, cot_ref, wg_ref, wu_ref, wd_ref, out_ref, inp_ref, part_ref, acc_g, acc_u, acc_d):
    step = pl.program_id(0)
    hidden_width = wg_ref.shape[1]

    @pl.when(step == 0)
    def _():
        acc_g[...] = jnp.zeros_like(acc_g)
        acc_u[...] = jnp.zeros_like(acc_u)
        acc_d[...] = jnp.zeros_like(acc_d)

    x = tok_ref[...]
    c = cot_ref[...]
    wg = wg_ref[...]
    wu = wu_ref[...]
    wd = wd_ref[...]
    gate_pre = jnp.dot(x, wg, preferred_element_type=jnp.float32)
    up_pre = jnp.dot(x, wu, preferred_element_type=jnp.float32)
    activated, silu_slope = silu_parts(gate_pre)
    hidden = (activated * up_pre).astype(jnp.bfloat16)
    out_ref[...] = jnp.dot(hidden, wd, preferred_element_type=jnp.float32).astype(out_ref.dtype)
    d_hidden = contract_cols(c, wd)
    d_up = (d_hidden * activated).astype(jnp.bfloat16)
    d_gate = (d_hidden * up_pre * silu_slope).astype(jnp.bfloat16)
    inp_ref[...] = (contract_cols(d_gate, wg) + contract_cols(d_up, wu)).astype(inp_ref.dtype)
    acc_g[...] += contract_rows(x, d_gate)
    acc_u[...] += contract_rows(x, d_up)
    acc_d[...] += contract_rows(c, hidden)

    @pl.when(step == pl.num_programs(0) - 1)
    def _():
        part_ref[0] = acc_g[...].astype(part_ref.dtype)
        part_ref[1] = acc_u[...].astype(part_ref.dtype)
        part_ref[2] = acc_d[...].astype(part_ref.dtype)


def arm_math(tokens, cot, wg, wu, wd):
    rows, width = tokens.shape
    hidden_width = wg.shape[1]
    block = 512
    row_spec = pl.BlockSpec((block, width), lambda i: (i, 0))
    whole = lambda shape: pl.BlockSpec(shape, lambda i: (0, 0))
    flops = 2 * rows * width * hidden_width * 9
    return pl.pallas_call(
        arm_kernel,
        grid=(rows // block,),
        in_specs=[row_spec, row_spec, whole(wg.shape), whole(wu.shape), whole(wd.shape)],
        out_specs=[
            row_spec,
            row_spec,
            pl.BlockSpec((3, width, hidden_width), lambda i: (0, 0, 0)),
        ],
        out_shape=[
            jax.ShapeDtypeStruct((rows, width), jnp.bfloat16),
            jax.ShapeDtypeStruct((rows, width), jnp.bfloat16),
            jax.ShapeDtypeStruct((3, width, hidden_width), jnp.bfloat16),
        ],
        scratch_shapes=[
            pltpu.VMEM((width, hidden_width), jnp.float32),
            pltpu.VMEM((width, hidden_width), jnp.float32),
            pltpu.VMEM((width, hidden_width), jnp.float32),
        ],
        compiler_params=pltpu.CompilerParams(
            dimension_semantics=("arbitrary",), vmem_limit_bytes=48 * 1024 * 1024
        ),
        cost_estimate=pl.CostEstimate(
            flops=flops, bytes_accessed=2 * (4 * rows * width + 6 * width * hidden_width), transcendentals=rows * hidden_width
        ),
    )(tokens, cot, wg, wu, wd)


def split_kernel(summed_ref, gate_ref, up_ref, down_ref):
    gate_ref[...] = summed_ref[0]
    up_ref[...] = summed_ref[1]
    down_ref[...] = summed_ref[2].astype(jnp.float32).T.astype(down_ref.dtype)


def split_grads(summed):
    _, width, part = summed.shape
    vmem = pl.BlockSpec(memory_space=pltpu.VMEM)
    return pl.pallas_call(
        split_kernel,
        in_specs=[vmem],
        out_specs=[vmem, vmem, vmem],
        out_shape=[
            jax.ShapeDtypeStruct((width, part), summed.dtype),
            jax.ShapeDtypeStruct((width, part), summed.dtype),
            jax.ShapeDtypeStruct((part, width), summed.dtype),
        ],
    )(summed)


def on_device(tokens, codes, cotangent, w_gate, w_up, w_down):
    token_count, feature_width = tokens.shape
    local_arms = w_gate.shape[0]
    arm_count = local_arms * lax.axis_size("expert")
    capacity = 4 * token_count // arm_count
    flat_codes = codes.T.reshape(-1)
    arm_ids = jnp.arange(arm_count, dtype=jnp.int32)
    onehot = (flat_codes[:, None] == arm_ids[None, :]).astype(jnp.bfloat16)
    count = flat_codes.shape[0]
    before = (
        lax.broadcasted_iota(jnp.int32, (count, count), 1)
        < lax.broadcasted_iota(jnp.int32, (count, count), 0)
    ).astype(jnp.bfloat16)
    earlier = jnp.dot(before, onehot, preferred_element_type=jnp.float32)
    slot = jnp.sum(earlier * onehot.astype(jnp.float32), axis=1).astype(jnp.int32)
    tok_dest = flat_codes * (2 * capacity) + slot
    cot_dest = tok_dest + capacity
    cot_f = cotangent.astype(jnp.float32)
    sources = jnp.concatenate(
        [tokens, (cot_f * fact_share).astype(jnp.bfloat16), (cot_f * counter_share).astype(jnp.bfloat16)]
    )
    dest = jnp.concatenate([tok_dest, cot_dest])
    place = (
        lax.broadcasted_iota(jnp.int32, (arm_count * 2 * capacity, dest.shape[0]), 0) == dest[None, :]
    ).astype(jnp.bfloat16)
    place_in = jnp.concatenate(
        [place[:, :token_count] + place[:, token_count : 2 * token_count], place[:, 2 * token_count :]], axis=1
    )
    send = (
        jnp.dot(place_in, sources, preferred_element_type=jnp.float32)
        .astype(jnp.bfloat16)
        .reshape(arm_count, 2 * capacity, feature_width)
    )
    got = lax.all_to_all(send, "expert", 0, 0, tiled=True)
    arm_tokens = got[:, :capacity].reshape(1, -1, feature_width)
    arm_cot = got[:, capacity:].reshape(1, -1, feature_width)

    out_rows, input_rows, partials = arm_math(
        arm_tokens[0], arm_cot[0], w_gate[0], w_up[0], w_down[0]
    )
    ret = jnp.concatenate(
        [
            out_rows.reshape(-1, capacity, feature_width),
            input_rows.reshape(-1, capacity, feature_width),
        ],
        axis=1,
    )
    back = lax.all_to_all(ret, "expert", 0, 0, tiled=True).reshape(-1, feature_width)
    picked = lax.dot_general(
        place, back, (((0,), (0,)), ((), ())), preferred_element_type=jnp.float32
    ).reshape(4, token_count, feature_width)
    head_output = (fact_share * picked[0] + counter_share * picked[1]).astype(jnp.bfloat16)
    grad_tokens = (picked[2] + picked[3]).astype(jnp.bfloat16)

    summed = lax.psum_scatter(partials, "dp", scatter_dimension=2, tiled=True)
    grad_gate, grad_up, grad_down = (g[None] for g in split_grads(summed))
    return (head_output, grad_tokens, grad_gate, grad_up, grad_down)


def solution(mesh):
    return jax.shard_map(
        on_device,
        mesh=mesh,
        in_specs=(
            P(("dp", "expert"), None),
            P(("dp", "expert"), None),
            P(("dp", "expert"), None),
            P("expert", None, None),
            P("expert", None, None),
            P("expert", None, None),
        ),
        out_specs=(
            P(("dp", "expert"), None),
            P(("dp", "expert"), None),
            P("expert", None, "dp"),
            P("expert", None, "dp"),
            P("expert", "dp", None),
        ),
        check_vma=False,
    )
```

```python
import functools

import jax
import jax.numpy as jnp
from jax import lax
from jax.experimental import pallas as pl
from jax.experimental.pallas import tpu as pltpu
from jax.sharding import PartitionSpec as P

fact_share = 0.7
counter_share = 0.3
MESH_ID = pl.DeviceIdType.MESH


def silu_parts(gate_pre):
    sigmoid_gate = jax.nn.sigmoid(gate_pre)
    return (gate_pre * sigmoid_gate, sigmoid_gate * (1.0 + gate_pre * (1.0 - sigmoid_gate)))


def exchange_kernel(n, send_hbm, recv_hbm, send_sem, recv_sem, local_sem):
    me = lax.axis_index("expert")
    row = lax.axis_index("dp")

    def copy_to(i):
        j = lax.rem(me + i, n)
        return pltpu.make_async_remote_copy(
            src_ref=send_hbm.at[j],
            dst_ref=recv_hbm.at[me],
            send_sem=send_sem.at[j],
            recv_sem=recv_sem.at[me],
            device_id=(row, j),
            device_id_type=MESH_ID,
        )

    def start(i, carry):
        copy_to(i).start()
        return carry

    lax.fori_loop(1, n, start, 0)
    local = pltpu.make_async_copy(send_hbm.at[me], recv_hbm.at[me], local_sem)
    local.start()
    local.wait()

    def finish(i, carry):
        j = lax.rem(me + i, n)
        copy_to(i).wait_send()
        pltpu.make_async_remote_copy(
            src_ref=send_hbm.at[j],
            dst_ref=recv_hbm.at[j],
            send_sem=send_sem.at[j],
            recv_sem=recv_sem.at[j],
            device_id=(row, j),
            device_id_type=MESH_ID,
        ).wait_recv()
        return carry

    lax.fori_loop(1, n, finish, 0)


def exchange(send):
    n = send.shape[0]
    nbytes = send.size * send.dtype.itemsize
    return pl.pallas_call(
        functools.partial(exchange_kernel, n),
        out_shape=jax.ShapeDtypeStruct(send.shape, send.dtype),
        in_specs=[pl.BlockSpec(memory_space=pl.ANY)],
        out_specs=pl.BlockSpec(memory_space=pl.ANY),
        scratch_shapes=[
            pltpu.SemaphoreType.DMA((n,)),
            pltpu.SemaphoreType.DMA((n,)),
            pltpu.SemaphoreType.DMA,
        ],
        compiler_params=pltpu.CompilerParams(has_side_effects=True),
        cost_estimate=pl.CostEstimate(flops=0, bytes_accessed=2 * nbytes, transcendentals=0),
    )(send)


def contract_rows(a, b):
    return lax.dot_general(a, b, (((0,), (0,)), ((), ())), preferred_element_type=jnp.float32)


def contract_cols(a, b):
    return lax.dot_general(a, b, (((1,), (1,)), ((), ())), preferred_element_type=jnp.float32)


def arm_kernel(tok_ref, cot_ref, wg_ref, wu_ref, wd_ref, out_ref, inp_ref, part_ref, acc_g, acc_u, acc_d):
    step = pl.program_id(0)
    hidden_width = wg_ref.shape[1]

    @pl.when(step == 0)
    def _():
        acc_g[...] = jnp.zeros_like(acc_g)
        acc_u[...] = jnp.zeros_like(acc_u)
        acc_d[...] = jnp.zeros_like(acc_d)

    x = tok_ref[...]
    c = cot_ref[...]
    wg = wg_ref[...]
    wu = wu_ref[...]
    wd = wd_ref[...]
    gate_pre = jnp.dot(x, wg, preferred_element_type=jnp.float32)
    up_pre = jnp.dot(x, wu, preferred_element_type=jnp.float32)
    activated, silu_slope = silu_parts(gate_pre)
    hidden = (activated * up_pre).astype(jnp.bfloat16)
    out_ref[...] = jnp.dot(hidden, wd, preferred_element_type=jnp.float32).astype(out_ref.dtype)
    d_hidden = contract_cols(c, wd)
    d_up = (d_hidden * activated).astype(jnp.bfloat16)
    d_gate = (d_hidden * up_pre * silu_slope).astype(jnp.bfloat16)
    inp_ref[...] = (contract_cols(d_gate, wg) + contract_cols(d_up, wu)).astype(inp_ref.dtype)
    acc_g[...] += contract_rows(x, d_gate)
    acc_u[...] += contract_rows(x, d_up)
    acc_d[...] += contract_rows(c, hidden)

    @pl.when(step == pl.num_programs(0) - 1)
    def _():
        part_ref[0] = acc_g[...].astype(part_ref.dtype)
        part_ref[1] = acc_u[...].astype(part_ref.dtype)
        part_ref[2] = acc_d[...].astype(part_ref.dtype)


def arm_math(tokens, cot, wg, wu, wd):
    rows, width = tokens.shape
    hidden_width = wg.shape[1]
    block = 512
    row_spec = pl.BlockSpec((block, width), lambda i: (i, 0))
    whole = lambda shape: pl.BlockSpec(shape, lambda i: (0, 0))
    flops = 2 * rows * width * hidden_width * 9
    return pl.pallas_call(
        arm_kernel,
        grid=(rows // block,),
        in_specs=[row_spec, row_spec, whole(wg.shape), whole(wu.shape), whole(wd.shape)],
        out_specs=[
            row_spec,
            row_spec,
            pl.BlockSpec((3, width, hidden_width), lambda i: (0, 0, 0)),
        ],
        out_shape=[
            jax.ShapeDtypeStruct((rows, width), jnp.bfloat16),
            jax.ShapeDtypeStruct((rows, width), jnp.bfloat16),
            jax.ShapeDtypeStruct((3, width, hidden_width), jnp.bfloat16),
        ],
        scratch_shapes=[
            pltpu.VMEM((width, hidden_width), jnp.float32),
            pltpu.VMEM((width, hidden_width), jnp.float32),
            pltpu.VMEM((width, hidden_width), jnp.float32),
        ],
        compiler_params=pltpu.CompilerParams(
            dimension_semantics=("arbitrary",), vmem_limit_bytes=48 * 1024 * 1024
        ),
        cost_estimate=pl.CostEstimate(
            flops=flops, bytes_accessed=2 * (4 * rows * width + 6 * width * hidden_width), transcendentals=rows * hidden_width
        ),
    )(tokens, cot, wg, wu, wd)


def split_kernel(summed_ref, gate_ref, up_ref, down_ref):
    gate_ref[...] = summed_ref[0]
    up_ref[...] = summed_ref[1]
    down_ref[...] = summed_ref[2].astype(jnp.float32).T.astype(down_ref.dtype)


def split_grads(summed):
    _, width, part = summed.shape
    vmem = pl.BlockSpec(memory_space=pltpu.VMEM)
    return pl.pallas_call(
        split_kernel,
        in_specs=[vmem],
        out_specs=[vmem, vmem, vmem],
        out_shape=[
            jax.ShapeDtypeStruct((width, part), summed.dtype),
            jax.ShapeDtypeStruct((width, part), summed.dtype),
            jax.ShapeDtypeStruct((part, width), summed.dtype),
        ],
    )(summed)


def pick_kernel(tokens, place_ref, back_ref, head_ref, grad_ref):
    picked = contract_rows(place_ref[...], back_ref[...])
    head_ref[...] = (
        fact_share * picked[:tokens] + counter_share * picked[tokens : 2 * tokens]
    ).astype(head_ref.dtype)
    grad_ref[...] = (picked[2 * tokens : 3 * tokens] + picked[3 * tokens :]).astype(grad_ref.dtype)


def pick_back(place, back, tokens):
    vmem = pl.BlockSpec(memory_space=pltpu.VMEM)
    row = jax.ShapeDtypeStruct((tokens, back.shape[1]), jnp.bfloat16)
    return pl.pallas_call(
        functools.partial(pick_kernel, tokens),
        in_specs=[vmem, vmem],
        out_specs=[vmem, vmem],
        out_shape=[row, row],
    )(place, back)


def on_device(tokens, codes, cotangent, w_gate, w_up, w_down):
    token_count, feature_width = tokens.shape
    local_arms = w_gate.shape[0]
    arm_count = local_arms * lax.axis_size("expert")
    capacity = 4 * token_count // arm_count
    flat_codes = codes.T.reshape(-1)
    arm_ids = jnp.arange(arm_count, dtype=jnp.int32)
    onehot = (flat_codes[:, None] == arm_ids[None, :]).astype(jnp.bfloat16)
    count = flat_codes.shape[0]
    before = (
        lax.broadcasted_iota(jnp.int32, (count, count), 1)
        < lax.broadcasted_iota(jnp.int32, (count, count), 0)
    ).astype(jnp.bfloat16)
    earlier = jnp.dot(before, onehot, preferred_element_type=jnp.float32)
    slot = jnp.sum(earlier * onehot.astype(jnp.float32), axis=1).astype(jnp.int32)
    tok_dest = flat_codes * (2 * capacity) + slot
    cot_dest = tok_dest + capacity
    cot_f = cotangent.astype(jnp.float32)
    sources = jnp.concatenate(
        [tokens, (cot_f * fact_share).astype(jnp.bfloat16), (cot_f * counter_share).astype(jnp.bfloat16)]
    )
    dest = jnp.concatenate([tok_dest, cot_dest])
    place = (
        lax.broadcasted_iota(jnp.int32, (arm_count * 2 * capacity, dest.shape[0]), 0) == dest[None, :]
    ).astype(jnp.bfloat16)
    place_in = jnp.concatenate(
        [place[:, :token_count] + place[:, token_count : 2 * token_count], place[:, 2 * token_count :]], axis=1
    )
    send = (
        jnp.dot(place_in, sources, preferred_element_type=jnp.float32)
        .astype(jnp.bfloat16)
        .reshape(arm_count, 2 * capacity, feature_width)
    )
    got = lax.all_to_all(send, "expert", 0, 0, tiled=True)
    arm_tokens = got[:, :capacity].reshape(1, -1, feature_width)
    arm_cot = got[:, capacity:].reshape(1, -1, feature_width)

    out_rows, input_rows, partials = arm_math(
        arm_tokens[0], arm_cot[0], w_gate[0], w_up[0], w_down[0]
    )
    ret = jnp.concatenate(
        [
            out_rows.reshape(-1, capacity, feature_width),
            input_rows.reshape(-1, capacity, feature_width),
        ],
        axis=1,
    )
    back = lax.all_to_all(ret, "expert", 0, 0, tiled=True).reshape(-1, feature_width)
    head_output, grad_tokens = pick_back(place, back, token_count)

    summed = lax.psum_scatter(partials, "dp", scatter_dimension=2, tiled=True)
    grad_gate, grad_up, grad_down = (g[None] for g in split_grads(summed))
    return (head_output, grad_tokens, grad_gate, grad_up, grad_down)


def solution(mesh):
    return jax.shard_map(
        on_device,
        mesh=mesh,
        in_specs=(
            P(("dp", "expert"), None),
            P(("dp", "expert"), None),
            P(("dp", "expert"), None),
            P("expert", None, None),
            P("expert", None, None),
            P("expert", None, None),
        ),
        out_specs=(
            P(("dp", "expert"), None),
            P(("dp", "expert"), None),
            P("expert", None, "dp"),
            P("expert", None, "dp"),
            P("expert", "dp", None),
        ),
        check_vma=False,
    )
```

```python
import functools

import jax
import jax.numpy as jnp
from jax import lax
from jax.experimental import pallas as pl
from jax.experimental.pallas import tpu as pltpu
from jax.sharding import PartitionSpec as P

fact_share = 0.7
counter_share = 0.3
MESH_ID = pl.DeviceIdType.MESH


def silu_parts(gate_pre):
    sigmoid_gate = jax.nn.sigmoid(gate_pre)
    return (gate_pre * sigmoid_gate, sigmoid_gate * (1.0 + gate_pre * (1.0 - sigmoid_gate)))


def exchange_kernel(n, send_hbm, recv_hbm, send_sem, recv_sem, local_sem):
    me = lax.axis_index("expert")
    row = lax.axis_index("dp")

    def copy_to(i):
        j = lax.rem(me + i, n)
        return pltpu.make_async_remote_copy(
            src_ref=send_hbm.at[j],
            dst_ref=recv_hbm.at[me],
            send_sem=send_sem.at[j],
            recv_sem=recv_sem.at[me],
            device_id=(row, j),
            device_id_type=MESH_ID,
        )

    def start(i, carry):
        copy_to(i).start()
        return carry

    lax.fori_loop(1, n, start, 0)
    local = pltpu.make_async_copy(send_hbm.at[me], recv_hbm.at[me], local_sem)
    local.start()
    local.wait()

    def finish(i, carry):
        j = lax.rem(me + i, n)
        copy_to(i).wait_send()
        pltpu.make_async_remote_copy(
            src_ref=send_hbm.at[j],
            dst_ref=recv_hbm.at[j],
            send_sem=send_sem.at[j],
            recv_sem=recv_sem.at[j],
            device_id=(row, j),
            device_id_type=MESH_ID,
        ).wait_recv()
        return carry

    lax.fori_loop(1, n, finish, 0)


def exchange(send):
    n = send.shape[0]
    nbytes = send.size * send.dtype.itemsize
    return pl.pallas_call(
        functools.partial(exchange_kernel, n),
        out_shape=jax.ShapeDtypeStruct(send.shape, send.dtype),
        in_specs=[pl.BlockSpec(memory_space=pl.ANY)],
        out_specs=pl.BlockSpec(memory_space=pl.ANY),
        scratch_shapes=[
            pltpu.SemaphoreType.DMA((n,)),
            pltpu.SemaphoreType.DMA((n,)),
            pltpu.SemaphoreType.DMA,
        ],
        compiler_params=pltpu.CompilerParams(has_side_effects=True),
        cost_estimate=pl.CostEstimate(flops=0, bytes_accessed=2 * nbytes, transcendentals=0),
    )(send)


def contract_rows(a, b):
    return lax.dot_general(a, b, (((0,), (0,)), ((), ())), preferred_element_type=jnp.float32)


def contract_cols(a, b):
    return lax.dot_general(a, b, (((1,), (1,)), ((), ())), preferred_element_type=jnp.float32)


def arm_kernel(tok_ref, cot_ref, wg_ref, wu_ref, wd_ref, out_ref, inp_ref, part_ref):
    x = tok_ref[...]
    c = cot_ref[...]
    wg = wg_ref[...]
    wu = wu_ref[...]
    wd = wd_ref[...]
    gate_pre = jnp.dot(x, wg, preferred_element_type=jnp.float32)
    up_pre = jnp.dot(x, wu, preferred_element_type=jnp.float32)
    activated, silu_slope = silu_parts(gate_pre)
    hidden = (activated * up_pre).astype(jnp.bfloat16)
    out_ref[...] = jnp.dot(hidden, wd, preferred_element_type=jnp.float32).astype(out_ref.dtype)
    d_hidden = contract_cols(c, wd)
    d_up = (d_hidden * activated).astype(jnp.bfloat16)
    d_gate = (d_hidden * up_pre * silu_slope).astype(jnp.bfloat16)
    inp_ref[...] = (contract_cols(d_gate, wg) + contract_cols(d_up, wu)).astype(inp_ref.dtype)
    part_ref[0] = contract_rows(x, d_gate).astype(part_ref.dtype)
    part_ref[1] = contract_rows(x, d_up).astype(part_ref.dtype)
    part_ref[2] = contract_rows(c, hidden).astype(part_ref.dtype)


def arm_math(tokens, cot, wg, wu, wd):
    rows, width = tokens.shape
    hidden_width = wg.shape[1]
    block = rows
    row_spec = pl.BlockSpec((block, width), lambda i: (i, 0))
    whole = lambda shape: pl.BlockSpec(shape, lambda i: (0, 0))
    flops = 2 * rows * width * hidden_width * 9
    return pl.pallas_call(
        arm_kernel,
        grid=(rows // block,),
        in_specs=[row_spec, row_spec, whole(wg.shape), whole(wu.shape), whole(wd.shape)],
        out_specs=[
            row_spec,
            row_spec,
            pl.BlockSpec((3, width, hidden_width), lambda i: (0, 0, 0)),
        ],
        out_shape=[
            jax.ShapeDtypeStruct((rows, width), jnp.bfloat16),
            jax.ShapeDtypeStruct((rows, width), jnp.bfloat16),
            jax.ShapeDtypeStruct((3, width, hidden_width), jnp.bfloat16),
        ],
        compiler_params=pltpu.CompilerParams(
            dimension_semantics=("arbitrary",), vmem_limit_bytes=48 * 1024 * 1024
        ),
        cost_estimate=pl.CostEstimate(
            flops=flops, bytes_accessed=2 * (4 * rows * width + 6 * width * hidden_width), transcendentals=rows * hidden_width
        ),
    )(tokens, cot, wg, wu, wd)


def split_kernel(summed_ref, gate_ref, up_ref, down_ref):
    gate_ref[...] = summed_ref[0]
    up_ref[...] = summed_ref[1]
    down_ref[...] = summed_ref[2].astype(jnp.float32).T.astype(down_ref.dtype)


def split_grads(summed):
    _, width, part = summed.shape
    vmem = pl.BlockSpec(memory_space=pltpu.VMEM)
    return pl.pallas_call(
        split_kernel,
        in_specs=[vmem],
        out_specs=[vmem, vmem, vmem],
        out_shape=[
            jax.ShapeDtypeStruct((width, part), summed.dtype),
            jax.ShapeDtypeStruct((width, part), summed.dtype),
            jax.ShapeDtypeStruct((part, width), summed.dtype),
        ],
    )(summed)


def on_device(tokens, codes, cotangent, w_gate, w_up, w_down):
    token_count, feature_width = tokens.shape
    local_arms = w_gate.shape[0]
    arm_count = local_arms * lax.axis_size("expert")
    capacity = 4 * token_count // arm_count
    flat_codes = codes.T.reshape(-1)
    arm_ids = jnp.arange(arm_count, dtype=jnp.int32)
    onehot = (flat_codes[:, None] == arm_ids[None, :]).astype(jnp.bfloat16)
    count = flat_codes.shape[0]
    before = (
        lax.broadcasted_iota(jnp.int32, (count, count), 1)
        < lax.broadcasted_iota(jnp.int32, (count, count), 0)
    ).astype(jnp.bfloat16)
    earlier = jnp.dot(before, onehot, preferred_element_type=jnp.float32)
    slot = jnp.sum(earlier * onehot.astype(jnp.float32), axis=1).astype(jnp.int32)
    tok_dest = flat_codes * (2 * capacity) + slot
    cot_dest = tok_dest + capacity
    cot_f = cotangent.astype(jnp.float32)
    sources = jnp.concatenate(
        [tokens, (cot_f * fact_share).astype(jnp.bfloat16), (cot_f * counter_share).astype(jnp.bfloat16)]
    )
    dest = jnp.concatenate([tok_dest, cot_dest])
    place = (
        lax.broadcasted_iota(jnp.int32, (arm_count * 2 * capacity, dest.shape[0]), 0) == dest[None, :]
    ).astype(jnp.bfloat16)
    place_in = jnp.concatenate(
        [place[:, :token_count] + place[:, token_count : 2 * token_count], place[:, 2 * token_count :]], axis=1
    )
    send = (
        jnp.dot(place_in, sources, preferred_element_type=jnp.float32)
        .astype(jnp.bfloat16)
        .reshape(arm_count, 2 * capacity, feature_width)
    )
    got = lax.all_to_all(send, "expert", 0, 0, tiled=True)
    arm_tokens = got[:, :capacity].reshape(1, -1, feature_width)
    arm_cot = got[:, capacity:].reshape(1, -1, feature_width)

    out_rows, input_rows, partials = arm_math(
        arm_tokens[0], arm_cot[0], w_gate[0], w_up[0], w_down[0]
    )
    ret = jnp.concatenate(
        [
            out_rows.reshape(-1, capacity, feature_width),
            input_rows.reshape(-1, capacity, feature_width),
        ],
        axis=1,
    )
    back = lax.all_to_all(ret, "expert", 0, 0, tiled=True).reshape(-1, feature_width)
    picked = lax.dot_general(
        place, back, (((0,), (0,)), ((), ())), preferred_element_type=jnp.float32
    ).reshape(4, token_count, feature_width)
    head_output = (fact_share * picked[0] + counter_share * picked[1]).astype(jnp.bfloat16)
    grad_tokens = (picked[2] + picked[3]).astype(jnp.bfloat16)

    summed = lax.psum_scatter(partials, "dp", scatter_dimension=2, tiled=True)
    grad_gate, grad_up, grad_down = (g[None] for g in split_grads(summed))
    return (head_output, grad_tokens, grad_gate, grad_up, grad_down)


def solution(mesh):
    return jax.shard_map(
        on_device,
        mesh=mesh,
        in_specs=(
            P(("dp", "expert"), None),
            P(("dp", "expert"), None),
            P(("dp", "expert"), None),
            P("expert", None, None),
            P("expert", None, None),
            P("expert", None, None),
        ),
        out_specs=(
            P(("dp", "expert"), None),
            P(("dp", "expert"), None),
            P("expert", None, "dp"),
            P("expert", None, "dp"),
            P("expert", "dp", None),
        ),
        check_vma=False,
    )
```
